512 devices in a mesh: grid: 128 (over y, z, core), tile: 4 (over x).
Axes of the slice: x: 4, y: 8, z: 8, core: 2. Of those that a mesh axis runs over, the one named last changes fastest.
Arguments:
- basis_values: bfloat16 [12288, 256, 128], P(('grid', 'tile')), may hold values from -6 to 6
- blocks: int32 [12288, 2], P(('grid', 'tile')), may hold values from 0 to 2, as said below
- counts: int32 [12288], P(('grid', 'tile')), may hold values from 1 to 256, as said below
- weighted_potential: float32 [12288, 256], P(('grid', 'tile')), may hold values from -0.12 to 0.12
- xc_kernel: float32 [12288, 256], P(('grid', 'tile')), may hold values from -0.002 to -0.0002
- occ_coef: bfloat16 [8192, 512], P('grid'), may hold values from -0.5 to 0.5
- virt_coef: bfloat16 [8192, 7680], P('grid', 'tile'), may hold values from -0.0625 to 0.0625
- occ_energy: float32 [512], replicated, may hold values from -2 to -0.5
- virt_energy: float32 [7680], P('tile'), may hold values from 0.3 to 8
Outputs:
- response_coef: bfloat16 [8192, 512], P('grid')
- response_potential: float32 [12288, 256], P(('grid', 'tile'))
The draws below stay inside these ranges and needn't reach their ends.
Inputs may be any that keep to these rules, and one draw needn't show every extreme that they name: Each row names 2 different blocks of the window of 3 blocks around the batch's region. The live points of batch b are its first counts[b] slots; every device holds at least one full batch.
All inputs are finite; a program needn't handle non-finite values.
Results may differ from the reference program's by a relative error of at most 0.0061.
Values may be sent and summed in bfloat16 or wider, within the bound.
A program may use at most 128 MiB of HBM per device.

```python
import math
import jax
import jax.numpy as jnp
from jax import lax

NB = 8192
NOCC = 512
BB = 64
KB = 2
PTS = 256
NBATCH = 24
NV = 7680
NBLK = 128
BLK = 1
BATCHES = 12288
N_GRID = 128
N_TILE = 4


def draw_blocks(key, part):
    keys = jax.random.split(jax.random.fold_in(key, 11), BATCHES)
    orders = jax.vmap(lambda single: jax.random.permutation(single, 3 * BLK))(keys)
    return orders[:, :KB].astype(jnp.int32)


def draw_counts(key, part):
    first_key, second_key, third_key = jax.random.split(jax.random.fold_in(key, 23), 3)
    groups = BATCHES // NBATCH
    caps = jax.random.randint(first_key, (groups,), PTS // 4, PTS + 1)
    cap_each = jnp.repeat(caps, NBATCH, total_repeat_length=BATCHES)
    lowest = jnp.maximum(cap_each // 2, 1)
    fraction = jax.random.randint(second_key, (BATCHES,), 0, 1 << 20)
    chosen = lowest + fraction * (cap_each - lowest + 1) // (1 << 20)
    picked = jax.random.randint(third_key, (groups,), 0, NBATCH)
    slot = jnp.arange(BATCHES, dtype=jnp.int32) % NBATCH
    full_slot = slot == jnp.repeat(picked, NBATCH, total_repeat_length=BATCHES)
    return jnp.where(full_slot, PTS, chosen).astype(jnp.int32)


def levels(own_key, shape, cuts, least, high):
    loudness, own = 1.0, jax.random.fold_in(own_key, 6)
    for dim, shards_of in cuts:
        steps = jnp.exp(jax.random.uniform(jax.random.fold_in(own, dim), (shards_of,), jnp.float32, least / len(cuts), high / len(cuts)))
        loudness = loudness * jnp.repeat(steps, shape[dim] // shards_of).reshape([-1 if axis == dim else 1 for axis in range(len(shape))])
    return loudness


def noise(rng, dims, deviation, limit, pieces=(), held_as=jnp.bfloat16):
    entries = jax.random.normal(rng, dims, jnp.float32) * deviation
    if len(pieces) > 0:
        entries = levels(rng, dims, pieces, -0.22, 0.18) * entries
    return jnp.clip(entries, min=-limit, max=limit).astype(held_as)


def setup_inputs(seed: int = 0) -> dict:
    seeds = jax.random.split(jax.random.key(seed), 10)
    return {
        "basis_values": noise(seeds[0], (BATCHES, PTS, KB * BB), 1.0, 6.0, ((0, 512),)),
        "blocks": draw_blocks(jax.random.fold_in(seeds[9], 71), 0),
        "counts": draw_counts(jax.random.fold_in(seeds[9], 71), 0),
        "weighted_potential": noise(seeds[3], (BATCHES, PTS), 0.02, 0.12, ((0, 512),), jnp.float32),
        "xc_kernel": jnp.clip(-0.002 + 0.0018000001 * jax.random.uniform(seeds[4], (BATCHES, PTS), jnp.float32) ** levels(seeds[4], (BATCHES, PTS), ((0, 512),), -0.2, 0.2), -0.002, -0.0002),
        "occ_coef": noise(seeds[5], (NB, NOCC), (KB * BB) ** -0.5, 0.5, ((0, 128),)),
        "virt_coef": noise(seeds[6], (NB, NV), NB ** -0.5, 0.0625, ((0, 128), (1, 4))),
        "occ_energy": jnp.clip(jax.random.uniform(seeds[7], (NOCC,), jnp.float32, -2.0, -0.5), -2.0, -0.5),
        "virt_energy": jnp.clip(jnp.exp(math.log(8.0) - 3.2834143 * jax.random.uniform(seeds[8], (NV,), jnp.float32) ** levels(seeds[8], (NV,), ((0, 4),), -0.2, 0.2)), 0.3, 8.0),
    }


def basis_rows(region, blocks_here):
    first_block = (region * BLK - BLK + blocks_here) % NBLK
    offsets = jnp.arange(BB, dtype=jnp.int32)
    rows_index = first_block[:, :, None] * BB + offsets[None, None, :]
    return rows_index.reshape(blocks_here.shape[0], KB * BB).astype(jnp.int32)


def reference(basis_values, blocks, counts, weighted_potential, xc_kernel, occ_coef, virt_coef, occ_energy, virt_energy):
    per_region = N_TILE * NBATCH
    values_split = basis_values.reshape(N_GRID, per_region, PTS, KB * BB)
    blocks_split = blocks.reshape(N_GRID, per_region, KB)
    counts_split = counts.reshape(N_GRID, per_region)
    potential_split = weighted_potential.reshape(N_GRID, per_region, PTS)
    kernel_split = xc_kernel.reshape(N_GRID, per_region, PTS)
    regions = jnp.arange(N_GRID, dtype=jnp.int32)
    point_index = jnp.arange(PTS, dtype=jnp.int32)
    occ_float = occ_coef.astype(jnp.float32)

    def integrate(ham_sum, inputs):
        region, values_here, blocks_here, counts_here, potential_here = inputs
        rows_index = basis_rows(region, blocks_here)
        values_float = values_here.astype(jnp.float32)
        occ_rows = occ_float[rows_index]
        occ_values = jnp.einsum("bpk,bko->bpo", values_float, occ_rows)
        live_mask = point_index[None, :] < counts_here[:, None]
        weights = jnp.where(live_mask, potential_here, jnp.zeros_like(potential_here))
        scaled = (weights[:, :, None] * occ_values).astype(jnp.bfloat16)
        scaled = lax.optimization_barrier(scaled).astype(jnp.float32)
        contrib = jnp.einsum("bpk,bpo->bko", values_float, scaled)
        ham_sum = ham_sum.at[rows_index.reshape(-1)].add(contrib.reshape(-1, NOCC))
        return ham_sum, None

    ham_sum, unused = lax.scan(integrate, jnp.zeros((NB, NOCC), jnp.float32),
                               (regions, values_split, blocks_split, counts_split, potential_split))
    ham_occ = ham_sum.astype(jnp.bfloat16)
    virt_ham = jnp.dot(virt_coef.T, ham_occ, preferred_element_type=jnp.float32)
    rotation = (virt_ham / (occ_energy[None, :] - virt_energy[:, None])).astype(jnp.bfloat16)
    response_coef = jnp.dot(virt_coef, rotation, preferred_element_type=jnp.float32).astype(jnp.bfloat16)
    coef_float = response_coef.astype(jnp.float32)

    def respond(carry, inputs):
        region, values_here, blocks_here, counts_here, kernel_here = inputs
        rows_index = basis_rows(region, blocks_here)
        values_float = values_here.astype(jnp.float32)
        occ_values = jnp.einsum("bpk,bko->bpo", values_float, occ_float[rows_index])
        resp_values = jnp.einsum("bpk,bko->bpo", values_float, coef_float[rows_index])
        density = 4.0 * jnp.sum(occ_values * resp_values, axis=2)
        live_mask = point_index[None, :] < counts_here[:, None]
        result = jnp.where(live_mask, kernel_here * density, jnp.zeros_like(density))
        return carry, result

    unused_carry, potential_out = lax.scan(respond, jnp.zeros((), jnp.float32),
                                           (regions, values_split, blocks_split, counts_split, kernel_split))
    return response_coef, potential_out.reshape(BATCHES, PTS)
```

```python
import functools

import jax
import jax.numpy as jnp
from jax import lax
from jax.experimental import pallas as pl
from jax.experimental.pallas import tpu as pltpu
from jax.sharding import PartitionSpec as P

MESH = pl.DeviceIdType.MESH
B16 = jnp.bfloat16
F32 = jnp.float32
HAM_LINK = jnp.bfloat16
VIRT_LINK = jnp.bfloat16
COEF_LINK = jnp.bfloat16
NT = (((1,), (1,)), ((), ()))
NN = (((1,), (0,)), ((), ()))
BLK = 64
WIN = 256
SL = 64


def dot(a, b, dims=NN):
    return lax.dot_general(a, b, dims, preferred_element_type=F32)


def split(a):
    high = a.astype(B16)
    return high, (a - high.astype(F32)).astype(B16)


def kernel(
    topo, basis, blocks, counts, wpot, xc, occ, virt, eocc, evirt,
    coef_out, pot_out,
    occw, occt, bw, mat, ps, rb, hz, v2, evb, eot, ws, wr, rz, cs, cr, cw,
    sa, ra, sv1, rv1, sv2, rv2, svf, rvf, sv3, rv3, se, re,
    sb, rbs, sh, rh, sw, rw, sr, rr, sc, rc, sd, rd,
):
    nx, ny, nz = topo
    nq = ny * nz
    wy = 4 * WIN // ny
    g = lax.axis_index("grid")
    t = lax.axis_index("tile")
    c = g % 2
    q = g // 2
    z = q % nz
    y = q // nz
    gother = (g + 2 * nq - 1 + 2 * c) % (2 * nq)
    qup = (q + 1) % nq
    qdown = (q + nq - 1) % nq
    qother = (q + nq - 1 + 2 * c) % nq
    s_me = t * 2 + c
    nbatch = basis.shape[0]
    pending = []

    def zring(d):
        zz = (z + d) % nz
        return zz, 2 * (y * nz + zz) + c

    def yring(d):
        yy = (y + d) % ny
        return yy, 2 * (yy * nz + z) + c

    def push(src, dst, send, recv, gg, tt):
        copy = pltpu.make_async_remote_copy(
            src_ref=src, dst_ref=dst, send_sem=send, recv_sem=recv,
            device_id=(gg, tt), device_id_type=MESH,
        )
        copy.start()
        pending.append(copy)

    def arrive(dst, send, recv, gg, tt):
        pltpu.make_async_remote_copy(
            src_ref=dst, dst_ref=dst, send_sem=send, recv_sem=recv,
            device_id=(gg, tt), device_id_type=MESH,
        ).wait_recv()

    def vstart(zz):
        return pl.multiple_of(WIN * zz - 128 * (zz // (nz - 1)), 128)

    bar = pltpu.get_barrier_semaphore()
    own_chip = [(dc, dt) for dc in range(2) for dt in range(nx) if (dc, dt) != (0, 0)]
    for dc, dt in own_chip:
        pl.semaphore_signal(
            bar, inc=1, device_id=(2 * q + (c + dc) % 2, (t + dt) % nx), device_id_type=MESH
        )
    for qq in (qup, qdown):
        for cc in range(2):
            for tt in range(nx):
                pl.semaphore_signal(bar, inc=1, device_id=(2 * qq + cc, tt), device_id_type=MESH)
    for d in range(1, nz):
        pl.semaphore_signal(bar, inc=1, device_id=(zring(d)[1], t), device_id_type=MESH)
    for d in range(1, ny):
        pl.semaphore_signal(bar, inc=1, device_id=(yring(d)[1], t), device_id_type=MESH)

    mat[...] = jnp.zeros_like(mat)
    occw[pl.ds(pl.multiple_of(BLK * c, BLK), BLK), :] = occ[...]
    occw[pl.ds(pl.multiple_of(128 + BLK * c, BLK), BLK), :] = jnp.zeros((BLK, 512), B16)
    v2[t, z, c] = virt[:, pl.ds(vstart(z), WIN)]
    evb[:, pl.ds(pl.multiple_of(WIN * t, WIN), WIN)] = jnp.broadcast_to(
        evirt[:, pl.ds(vstart(z), WIN)], (8, WIN)
    )
    eot[...] = jnp.transpose(jnp.broadcast_to(eocc[...], (128, 512)))

    pl.semaphore_wait(bar, len(own_chip) + 4 * nx + nz - 1 + ny - 1)

    own_rows = pl.ds(pl.multiple_of(BLK * c, BLK), BLK)
    far_rows = pl.ds(pl.multiple_of(128 + BLK * c, BLK), BLK)
    sib = 2 * q + 1 - c
    push(occ, occw.at[own_rows], sa.at[0], ra.at[0], sib, t)
    push(occ, occw.at[far_rows], sa.at[1], ra.at[1], gother, t)
    for d in range(1, nz):
        zz, gg = zring(d)
        push(virt.at[:, pl.ds(vstart(zz), WIN)], v2.at[t, z, c], sv1.at[d], rv1.at[d], gg, t)
    mine_e = evb.at[:, pl.ds(pl.multiple_of(WIN * t, WIN), WIN)]
    for d in range(1, nx):
        push(mine_e, mine_e, se.at[d], re.at[d], g, (t + d) % nx)

    row = lax.broadcasted_iota(jnp.int32, (WIN, 128), 0)
    col = lax.broadcasted_iota(jnp.int32, (WIN, 128), 1)
    lane = lax.broadcasted_iota(jnp.int32, (1, WIN), 1)

    def integrate(b, carry):
        first = (BLK * (blocks[0, b] + c + 3)) % WIN
        second = (BLK * (blocks[1, b] + c + 3)) % WIN
        target = jnp.where(col < BLK, col + first, col - BLK + second)
        pick = jnp.where(row == target, 1.0, 0.0).astype(B16)
        spread = dot(pick, basis[b], NT)
        wide = spread.astype(B16)
        bw[b] = wide
        weight = jnp.where(lane < counts[0, b], wpot[pl.ds(b, 1), :], 0.0)
        mat[...] += dot((spread * weight).astype(B16), wide, NT)
        return carry

    lax.fori_loop(0, nbatch, integrate, 0)

    arrive(occw.at[pl.ds(pl.multiple_of(BLK * (1 - c), BLK), BLK)], sa.at[0], ra.at[0], sib, t)
    arrive(occw.at[pl.ds(pl.multiple_of(192 - BLK * c, BLK), BLK)], sa.at[1], ra.at[1], gother, t)
    occt[...] = jnp.transpose(occw[...].astype(F32)).astype(B16)
    high, low = split(mat[...])
    part = dot(occt[...], high) + dot(occt[...], low)
    for s in range(2 * nx):
        for h in range(2):
            ps[s, h] = part[SL * s : SL * s + SL, 128 * h : 128 * h + 128].astype(HAM_LINK)

    slot = 4 * c + t
    rb[slot] = ps[s_me, 0]
    for n, (dc, dt) in enumerate(own_chip):
        cc, tt = (c + dc) % 2, (t + dt) % nx
        push(ps.at[tt * 2 + cc, 0], rb.at[slot], sb.at[n], rbs.at[slot], 2 * q + cc, tt)
    for cc in range(2):
        for tt in range(nx):
            push(ps.at[tt * 2 + cc, 1], rb.at[8 + slot], sb.at[8 + 4 * cc + tt], rbs.at[8 + slot],
                 2 * qother + cc, tt)

    for d in range(1, nz):
        zz = (z + nz - d) % nz
        arrive(v2.at[t, zz, c], sv1.at[d], rv1.at[d], zring(nz - d)[1], t)
    right, left = (t + 1) % nx, (t + nx - 1) % nx
    push(v2.at[t, :, c], v2.at[t, :, c], sv2.at[0], rv2.at[0], g, right)
    push(v2.at[t, :, c], v2.at[t, :, c], sv2.at[1], rv2.at[1], g, left)
    push(v2.at[t, :, c], v2.at[t, :, c], sv3.at[0], rv3.at[0], sib, t)

    for dc, dt in own_chip:
        cc, tt = (c + dc) % 2, (t + dt) % nx
        k = 4 * cc + tt
        arrive(rb.at[k], sb.at[0], rbs.at[k], 2 * q + cc, tt)
    for tt in range(nx):
        arrive(rb.at[8 + tt], sb.at[0], rbs.at[8 + tt], 2 * qup, tt)
        arrive(rb.at[12 + tt], sb.at[0], rbs.at[12 + tt], 2 * qdown + 1, tt)
    ham = rb[0].astype(F32)
    for k in range(1, 16):
        ham = ham + rb[k].astype(F32)
    zcols = lambda zz: pl.ds(pl.multiple_of(128 * zz, 128), 128)
    hz[:, zcols(z)] = ham.astype(B16)
    for d in range(1, nz):
        push(hz.at[:, zcols(z)], hz.at[:, zcols(z)], sh.at[d], rh.at[d], zring(d)[1], t)

    half = nz // 2
    arrive(v2.at[left, :, c], sv2.at[0], rv2.at[0], g, left)
    push(v2.at[left, 0:half, c], v2.at[left, 0:half, c], svf.at[0], rvf.at[0], g, right)
    push(v2.at[left, :, c], v2.at[left, :, c], sv3.at[1], rv3.at[1], sib, t)
    arrive(v2.at[right, :, c], sv2.at[1], rv2.at[1], g, right)
    push(v2.at[right, half:nz, c], v2.at[right, half:nz, c], svf.at[1], rvf.at[1], g, left)
    push(v2.at[right, :, c], v2.at[right, :, c], sv3.at[2], rv3.at[2], sib, t)
    across = (t + 2) % nx
    arrive(v2.at[across, 0:half, c], svf.at[0], rvf.at[0], g, left)
    arrive(v2.at[across, half:nz, c], svf.at[1], rvf.at[1], g, right)
    push(v2.at[across, :, c], v2.at[across, :, c], sv3.at[3], rv3.at[3], sib, t)
    for d in range(1, nz):
        arrive(hz.at[:, zcols((z + nz - d) % nz)], sh.at[d], rh.at[d], zring(nz - d)[1], t)
    for n, tt in enumerate((t, left, right, across)):
        arrive(v2.at[tt, :, 1 - c], sv3.at[n], rv3.at[n], sib, t)

    for tt in range(nx):
        part = dot(hz[...], v2[tt].reshape(nz * 128, WIN))
        for j in range(WIN // 128):
            at = 128 * (2 * tt + j)
            ws[at // wy, :, at % wy : at % wy + 128] = part[:, 128 * j : 128 * j + 128].astype(VIRT_LINK)
    wr[y] = ws[y]
    for d in range(1, ny):
        yy, gg = yring(d)
        push(ws.at[yy], wr.at[y], sw.at[d], rw.at[d], gg, t)
    for d in range(1, nx):
        tt = (t + nx - d) % nx
        theirs = evb.at[:, pl.ds(pl.multiple_of(WIN * tt, WIN), WIN)]
        arrive(theirs, se.at[d], re.at[d], g, tt)
    for d in range(1, ny):
        arrive(wr.at[(y + ny - d) % ny], sw.at[d], rw.at[d], yring(ny - d)[1], t)
    total = wr[0].astype(F32)
    for k in range(1, ny):
        total = total + wr[k].astype(F32)
    ycols = lambda yy: pl.ds(pl.multiple_of(wy * yy, 128), wy)
    gap = eot[pl.ds(pl.multiple_of(SL * s_me, SL), SL), 0:1] - evb[0:1, ycols(y)]
    place = lax.broadcasted_iota(jnp.int32, (SL, wy), 1) + wy * y
    repeat = jnp.logical_and(place % WIN < 128 * (z // (nz - 1)), place >= 0)
    rz[:, ycols(y)] = jnp.where(repeat, 0.0, total / gap).astype(B16)
    for d in range(1, ny):
        push(rz.at[:, ycols(y)], rz.at[:, ycols(y)], sr.at[d], rr.at[d], yring(d)[1], t)
    for d in range(1, ny):
        arrive(rz.at[:, ycols((y + ny - d) % ny)], sr.at[d], rr.at[d], yring(ny - d)[1], t)

    coef = dot(rz[:, 0:WIN], v2[0].reshape(nz * 128, WIN), NT)
    for tt in range(1, nx):
        coef += dot(rz[:, WIN * tt : WIN * tt + WIN], v2[tt].reshape(nz * 128, WIN), NT)
    for k in range(nz):
        cs[k] = coef[:, 128 * k : 128 * k + 128].astype(COEF_LINK)
    cr[z] = cs[z]
    for d in range(1, nz):
        zz, gg = zring(d)
        push(cs.at[zz], cr.at[z], sc.at[d], rc.at[d], gg, t)
    for d in range(1, nz):
        arrive(cr.at[(z + nz - d) % nz], sc.at[d], rc.at[d], zring(nz - d)[1], t)
    done = cr[0].astype(F32)
    for k in range(1, nz):
        done = done + cr[k].astype(F32)
    cw[0, s_me] = done.astype(B16)

    for n, (dc, dt) in enumerate(own_chip):
        push(cw.at[0, s_me], cw.at[0, s_me], sd.at[n], rd.at[0, s_me],
             2 * q + (c + dc) % 2, (t + dt) % nx)
    for tt in range(nx):
        push(cw.at[0, s_me], cw.at[1, s_me], sd.at[8 + tt], rd.at[1, s_me], 2 * qup, tt)
        push(cw.at[0, s_me], cw.at[1, s_me], sd.at[12 + tt], rd.at[1, s_me], 2 * qdown + 1, tt)
    for dc, dt in own_chip:
        cc, tt = (c + dc) % 2, (t + dt) % nx
        k = tt * 2 + cc
        arrive(cw.at[0, k], sd.at[0], rd.at[0, k], 2 * q + cc, tt)
    for cc in range(2):
        for tt in range(nx):
            k = tt * 2 + cc
            arrive(cw.at[1, k], sd.at[0], rd.at[1, k], 2 * qother + cc, tt)

    near = cw[0].reshape(512, 128)
    far = cw[1].reshape(512, 128)
    krow = lax.broadcasted_iota(jnp.int32, (BLK, 128), 0)
    kcol = lax.broadcasted_iota(jnp.int32, (BLK, 128), 1)
    pick = jnp.where(kcol == krow + BLK * c, 1.0, 0.0).astype(B16)
    coef_out[...] = dot(pick, near, NT).astype(B16)
    mat[:, 0:128] = dot(occw[...], near)
    mat[:, 128:256] = dot(occw[...], far)
    high, low = split(mat[...])
    bw_low = low
    occt_high = occt.at[0:WIN, :]
    occt_low = occt.at[WIN : 2 * WIN, :]
    occt_high[...] = high
    occt_low[...] = bw_low

    def respond(b, carry):
        wide = bw[b]
        resp = dot(occt_high[...], wide) + dot(occt_low[...], wide)
        density = 4.0 * jnp.sum(resp * wide.astype(F32), axis=0, keepdims=True)
        value = xc[pl.ds(b, 1), :] * density
        pot_out[pl.ds(b, 1), :] = jnp.where(lane < counts[0, b], value, 0.0)
        return carry

    lax.fori_loop(0, nbatch, respond, 0)
    for copy in pending:
        copy.wait_send()


def per_device(topo, basis, blocks, counts, wpot, xc, occ, virt, eocc, evirt):
    nx, ny, nz = topo
    nbatch, points, columns = basis.shape
    rows, nocc = occ.shape
    wy = 4 * WIN // ny
    vmem = pl.BlockSpec(memory_space=pltpu.VMEM)
    smem = pl.BlockSpec(memory_space=pltpu.SMEM)
    dma = pltpu.SemaphoreType.DMA
    scratch = [
        pltpu.VMEM((WIN, nocc), B16),
        pltpu.VMEM((nocc, WIN), B16),
        pltpu.VMEM((nbatch, WIN, points), B16),
        pltpu.VMEM((WIN, WIN), F32),
        pltpu.VMEM((8, 2, SL, 128), HAM_LINK),
        pltpu.VMEM((16, SL, 128), HAM_LINK),
        pltpu.VMEM((SL, 128 * nz), B16),
        pltpu.VMEM((nx, nz, 2, BLK, WIN), B16),
        pltpu.VMEM((8, nx * WIN), F32),
        pltpu.VMEM((nocc, 128), F32),
        pltpu.VMEM((ny, SL, wy), VIRT_LINK),
        pltpu.VMEM((ny, SL, wy), VIRT_LINK),
        pltpu.VMEM((SL, nx * WIN), B16),
        pltpu.VMEM((nz, SL, 128), COEF_LINK),
        pltpu.VMEM((nz, SL, 128), COEF_LINK),
        pltpu.VMEM((2, 8, SL, 128), B16),
        dma((2,)), dma((2,)),
        dma((nz,)), dma((nz,)),
        dma((2,)), dma((2,)),
        dma((2,)), dma((2,)),
        dma((4,)), dma((4,)),
        dma((nx,)), dma((nx,)),
        dma((16,)), dma((16,)),
        dma((nz,)), dma((nz,)),
        dma((ny,)), dma((ny,)),
        dma((ny,)), dma((ny,)),
        dma((nz,)), dma((nz,)),
        dma((16,)), dma((2, 8)),
    ]
    return pl.pallas_call(
        functools.partial(kernel, topo),
        out_shape=(
            jax.ShapeDtypeStruct((rows, nocc), B16),
            jax.ShapeDtypeStruct((nbatch, points), F32),
        ),
        in_specs=[vmem, smem, smem] + [vmem] * 6,
        out_specs=(vmem, vmem),
        scratch_shapes=scratch,
        compiler_params=pltpu.CompilerParams(collective_id=0, has_side_effects=True),
        name="dfpt_cycle",
    )(
        basis, blocks.T, counts.reshape(1, -1), wpot, xc, occ, virt,
        eocc.reshape(1, -1), evirt.reshape(1, -1),
    )


def solution(mesh):
    side = 1
    while 2 * side * side < mesh.shape["grid"]:
        side += 1
    topo = (mesh.shape["tile"], side, side)
    in_specs = (
        P(("grid", "tile"), None, None),
        P(("grid", "tile"), None),
        P(("grid", "tile")),
        P(("grid", "tile"), None),
        P(("grid", "tile"), None),
        P("grid", None),
        P("grid", "tile"),
        P(),
        P("tile"),
    )
    out_specs = (P("grid", None), P(("grid", "tile"), None))
    return jax.shard_map(
        functools.partial(per_device, topo),
        mesh=mesh, in_specs=in_specs, out_specs=out_specs, check_vma=False,
    )
```

```python
import functools

import jax
import jax.numpy as jnp
from jax import lax
from jax.experimental import pallas as pl
from jax.experimental.pallas import tpu as pltpu
from jax.sharding import PartitionSpec as P

MESH = pl.DeviceIdType.MESH
B16 = jnp.bfloat16
F32 = jnp.float32
HAM_LINK = jnp.bfloat16
VIRT_LINK = jnp.bfloat16
COEF_LINK = jnp.bfloat16
NT = (((1,), (1,)), ((), ()))
NN = (((1,), (0,)), ((), ()))
BLK = 64
WIN = 256
SL = 64
PER = 4


def dot(a, b, dims=NN):
    return lax.dot_general(a, b, dims, preferred_element_type=F32)


def split(a):
    high = a.astype(B16)
    return high, (a - high.astype(F32)).astype(B16)


def kernel(
    topo, basis_in, blocks_in, counts_in, wpot_in, occ, virt, eocc_in, evirt_in,
    coef_out, dens_out,
    blocks, counts, basis, wpot, eocc, evirt, coef, dens, gmat,
    occw, occt, bw, mat, ps, rb, hz, v2, evb, eot, ws, wr, rz, cs, cr, cw,
    sl, sa, ra, sv1, rv1, sv2, rv2, svf, rvf, sv3, rv3, se, re,
    sb, rbs, sh, rh, sw, rw, sr, rr, sc, rc, sd, rd,
):
    nx, ny, nz = topo
    nq = ny * nz
    wy = 4 * WIN // ny
    g = lax.axis_index("grid")
    t = lax.axis_index("tile")
    c = g % 2
    q = g // 2
    z = q % nz
    y = q // nz
    gother = (g + 2 * nq - 1 + 2 * c) % (2 * nq)
    qup = (q + 1) % nq
    qdown = (q + nq - 1) % nq
    qother = (q + nq - 1 + 2 * c) % nq
    s_me = t * 2 + c
    groups, _, span = bw.shape
    per = span // WIN
    nbatch = groups * per
    third = nbatch // 3

    def local(src, dst, sem):
        copy = pltpu.make_async_copy(src, dst, sem)
        copy.start()
        return copy

    def zring(d):
        zz = (z + d) % nz
        return zz, 2 * (y * nz + zz) + c

    def yring(d):
        yy = (y + d) % ny
        return yy, 2 * (yy * nz + z) + c

    def push(src, dst, send, recv, gg, tt):
        pltpu.make_async_remote_copy(
            src_ref=src, dst_ref=dst, send_sem=send, recv_sem=recv,
            device_id=(gg, tt), device_id_type=MESH,
        ).start()

    def bytes_of(ref, sem):
        pltpu.make_async_copy(ref, ref, sem).wait()

    def vstart(zz):
        return pl.multiple_of(WIN * zz - 128 * (zz // (nz - 1)), 128)

    def outward(n):
        return sorted(range(1, n), key=lambda d: (min(d, n - d), d))

    znear, ynear = outward(nz), outward(ny)
    zfar, yfar = znear[::-1], ynear[::-1]
    xnear = [0] + outward(nx)
    xfar = xnear[::-1]

    bar = pltpu.get_barrier_semaphore()
    own_chip = [(dc, dt) for dc in range(2) for dt in range(nx) if (dc, dt) != (0, 0)]
    for dc, dt in own_chip:
        pl.semaphore_signal(
            bar, inc=1, device_id=(2 * q + (c + dc) % 2, (t + dt) % nx), device_id_type=MESH
        )
    for qq in (qup, qdown):
        for cc in range(2):
            for tt in range(nx):
                pl.semaphore_signal(bar, inc=1, device_id=(2 * qq + cc, tt), device_id_type=MESH)
    for d in range(1, nz):
        pl.semaphore_signal(bar, inc=1, device_id=(zring(d)[1], t), device_id_type=MESH)
    for d in range(1, ny):
        pl.semaphore_signal(bar, inc=1, device_id=(yring(d)[1], t), device_id_type=MESH)

    own_rows = pl.ds(pl.multiple_of(BLK * c, BLK), BLK)
    far_rows = pl.ds(pl.multiple_of(128 + BLK * c, BLK), BLK)
    load_b = local(blocks_in, blocks, sl.at[8])
    load_n = local(counts_in, counts, sl.at[9])
    load_w = local(wpot_in, wpot, sl.at[3])
    loads = [
        local(basis_in.at[pl.ds(third * k, third)], basis.at[pl.ds(third * k, third)], sl.at[k])
        for k in range(3)
    ]
    load_o = local(occ, occw.at[own_rows], sl.at[5])
    load_v = local(virt.at[:, pl.ds(vstart(z), WIN)], v2.at[t, z, c], sl.at[4])
    load_eo = local(eocc_in, eocc, sl.at[6])
    load_ev = local(evirt_in, evirt, sl.at[7])
    mat[...] = jnp.zeros_like(mat)
    occw[far_rows, :] = jnp.zeros((BLK, occw.shape[1]), B16)

    pl.semaphore_wait(bar, len(own_chip) + 4 * nx + nz - 1 + ny - 1)

    sib = 2 * q + 1 - c
    push(occ, occw.at[far_rows], sa, ra.at[1], gother, t)
    push(occ, occw.at[own_rows], sa, ra.at[0], sib, t)
    for n, d in enumerate(znear, 1):
        zz, gg = zring(d)
        push(virt.at[:, pl.ds(vstart(zz), WIN)], v2.at[t, z, c], sv1, rv1.at[(n + 1) // 2], gg, t)
    right, left, across = (t + 1) % nx, (t + nx - 1) % nx, (t + 2) % nx
    load_v.wait()
    push(v2.at[t, z, c], v2.at[t, z, c], sv2.at[0], rv2.at[0, 0], g, right)
    push(v2.at[t, z, c], v2.at[t, z, c], sv2.at[1], rv2.at[1, 0], g, left)

    row = lax.broadcasted_iota(jnp.int32, (WIN, 128), 0)
    col = lax.broadcasted_iota(jnp.int32, (WIN, 128), 1)
    lane = lax.broadcasted_iota(jnp.int32, (1, WIN), 1)
    load_w.wait()
    load_b.wait()
    load_n.wait()

    def integrate(n, carry):
        wides, scaled = [], []
        for j in range(per):
            b = per * n + j
            first = (BLK * (blocks[0, b] + c + 3)) % WIN
            second = (BLK * (blocks[1, b] + c + 3)) % WIN
            target = jnp.where(col < BLK, col + first, col - BLK + second)
            pick = jnp.where(row == target, 1.0, 0.0).astype(B16)
            spread = dot(pick, basis[b], NT)
            wide = spread.astype(B16)
            bw[n, :, WIN * j : WIN * j + WIN] = wide
            weight = jnp.where(lane < counts[0, b], wpot[pl.ds(b, 1), :], 0.0)
            wides.append(wide)
            scaled.append((spread * weight).astype(B16))
        mat[...] += dot(jnp.concatenate(scaled, axis=1), jnp.concatenate(wides, axis=1), NT)
        return carry

    for k in range(3):
        loads[k].wait()
        lax.fori_loop(groups * k // 3, groups * (k + 1) // 3, integrate, 0)

    load_o.wait()
    bytes_of(occw.at[pl.ds(pl.multiple_of(BLK * (1 - c), BLK), BLK)], ra.at[0])
    bytes_of(occw.at[pl.ds(pl.multiple_of(192 - BLK * c, BLK), BLK)], ra.at[1])
    occt[...] = jnp.transpose(occw[...].astype(F32)).astype(B16)
    high, low = split(mat[...])
    part = dot(occt[...], high) + dot(occt[...], low)
    for s in range(2 * nx):
        for h in range(2):
            ps[s, h] = part[SL * s : SL * s + SL, 128 * h : 128 * h + 128].astype(HAM_LINK)

    slot = 4 * c + t
    rb[slot] = ps[s_me, 0]
    for dt in xfar:
        tt = (t + dt) % nx
        for cc in range(2):
            push(ps.at[tt * 2 + cc, 1], rb.at[8 + slot], sb, rbs,
                 2 * qother + cc, tt)
        for dc in range(2):
            if dc or dt:
                cc = (c + dc) % 2
                push(ps.at[tt * 2 + cc, 0], rb.at[slot], sb, rbs,
                     2 * q + cc, tt)

    load_eo.wait()
    load_ev.wait()
    eot[...] = jnp.transpose(jnp.broadcast_to(eocc[...], (128, eocc.shape[1])))
    evb[:, pl.ds(pl.multiple_of(WIN * t, WIN), WIN)] = jnp.broadcast_to(
        evirt[pl.ds(vstart(z), WIN)].reshape(1, WIN), (8, WIN)
    )
    mine_e = evb.at[:, pl.ds(pl.multiple_of(WIN * t, WIN), WIN)]
    for d in range(1, nx):
        push(mine_e, mine_e, se, re, g, (t + d) % nx)

    order = [0] + znear
    steps = [order[0:1]] + [order[n : n + 2] for n in range(1, nz, 2)]
    for n, ds in enumerate(steps):
        if n:
            bytes_of(v2.at[t, 0 : len(ds), c], rv1.at[n])
            for d in ds:
                mine = v2.at[t, (z + d) % nz, c]
                push(mine, mine, sv2.at[0], rv2.at[0, n], g, right)
                push(mine, mine, sv2.at[1], rv2.at[1, n], g, left)
    push(v2.at[t, :, c], v2.at[t, :, c], sv3, rv3, sib, t)

    bytes_of(rb.at[0:15], rbs)
    ham = rb[0].astype(F32)
    for k in range(1, 16):
        ham = ham + rb[k].astype(F32)
    zcols = lambda zz: pl.ds(pl.multiple_of(128 * zz, 128), 128)
    hz[:, zcols(z)] = ham.astype(B16)
    for d in zfar:
        push(hz.at[:, zcols(z)], hz.at[:, zcols(z)], sh, rh, zring(d)[1], t)

    for n, ds in enumerate(steps):
        for k, (frm, to) in enumerate(((left, right), (right, left))):
            bytes_of(v2.at[frm, 0 : len(ds), c], rv2.at[k, n])
            for m, d in enumerate(ds):
                if (m + (n > 0) * (len(ds) == 1)) % 2 == k:
                    theirs = v2.at[frm, (z + d) % nz, c]
                    push(theirs, theirs, svf, rvf, g, to)
    push(v2.at[left, :, c], v2.at[left, :, c], sv3, rv3, sib, t)
    push(v2.at[right, :, c], v2.at[right, :, c], sv3, rv3, sib, t)
    bytes_of(v2.at[across, :, c], rvf)
    push(v2.at[across, :, c], v2.at[across, :, c], sv3, rv3, sib, t)
    bytes_of(hz.at[:, 0 : 128 * (nz - 1)], rh)
    bytes_of(v2.at[:, :, 1 - c], rv3)

    for tt in range(nx):
        part = dot(hz[...], v2[tt].reshape(nz * 128, WIN))
        for j in range(WIN // 128):
            at = 128 * (2 * tt + j)
            ws[at // wy, :, at % wy : at % wy + 128] = part[:, 128 * j : 128 * j + 128].astype(VIRT_LINK)
    wr[y] = ws[y]
    for d in yfar:
        yy, gg = yring(d)
        push(ws.at[yy], wr.at[y], sw, rw, gg, t)
    bytes_of(evb.at[:, 0 : WIN * (nx - 1)], re)
    bytes_of(wr.at[0 : ny - 1], rw)
    total = wr[0].astype(F32)
    for k in range(1, ny):
        total = total + wr[k].astype(F32)
    ycols = lambda yy: pl.ds(pl.multiple_of(wy * yy, 128), wy)
    gap = eot[pl.ds(pl.multiple_of(SL * s_me, SL), SL), 0:1] - evb[0:1, ycols(y)]
    place = lax.broadcasted_iota(jnp.int32, (SL, wy), 1) + wy * y
    repeat = place % WIN < 128 * (z // (nz - 1))
    rz[:, ycols(y)] = jnp.where(repeat, 0.0, total / gap).astype(B16)
    for d in yfar:
        push(rz.at[:, ycols(y)], rz.at[:, ycols(y)], sr, rr, yring(d)[1], t)
    bytes_of(rz.at[:, 0 : wy * (ny - 1)], rr)

    part = dot(rz[:, 0:WIN], v2[0].reshape(nz * 128, WIN), NT)
    for tt in range(1, nx):
        part += dot(rz[:, WIN * tt : WIN * tt + WIN], v2[tt].reshape(nz * 128, WIN), NT)
    for k in range(nz):
        cs[k] = part[:, 128 * k : 128 * k + 128].astype(COEF_LINK)
    cr[z] = cs[z]
    for d in zfar:
        zz, gg = zring(d)
        push(cs.at[zz], cr.at[z], sc, rc, gg, t)
    bytes_of(cr.at[0 : nz - 1], rc)
    done = cr[0].astype(F32)
    for k in range(1, nz):
        done = done + cr[k].astype(F32)
    cw[0, s_me] = done.astype(B16)

    for dt in xfar:
        tt = (t + dt) % nx
        push(cw.at[0, s_me], cw.at[1, s_me], sd, rd.at[1], 2 * qup, tt)
        push(cw.at[0, s_me], cw.at[1, s_me], sd, rd.at[1], 2 * qdown + 1, tt)
        for dc in range(2):
            if dc or dt:
                push(cw.at[0, s_me], cw.at[0, s_me], sd, rd.at[0],
                     2 * q + (c + dc) % 2, tt)
    bytes_of(cw.at[0, 0:7], rd.at[0])
    near = cw[0].reshape(8 * SL, 128)
    krow = lax.broadcasted_iota(jnp.int32, (BLK, 128), 0)
    kcol = lax.broadcasted_iota(jnp.int32, (BLK, 128), 1)
    pick = jnp.where(kcol == krow + BLK * c, 1.0, 0.0).astype(B16)
    coef[...] = dot(pick, near, NT)
    give_c = local(coef, coef_out, sl.at[0])
    gmat[:, 0:128] = dot(occw[...], near).astype(B16)
    bytes_of(cw.at[1], rd.at[1])
    far = cw[1].reshape(8 * SL, 128)
    gmat[:, 128:256] = dot(occw[...], far).astype(B16)

    def respond(n, carry):
        wide = bw[n]
        resp = dot(gmat[...], wide)
        total = jnp.sum(resp * wide.astype(F32), axis=0, keepdims=True)
        for j in range(per):
            dens[pl.ds(per * n + j, 1), :] = 4.0 * total[:, WIN * j : WIN * j + WIN]
        return carry

    lax.fori_loop(0, groups, respond, 0)
    give_d = local(dens, dens_out, sl.at[1])
    bytes_of(occw.at[0:128], sa)
    bytes_of(v2.at[0, 0 : nz - 1, 0], sv1)
    bytes_of(v2.at[0, :, 0], sv2.at[0])
    bytes_of(v2.at[0, :, 0], sv2.at[1])
    bytes_of(v2.at[0, :, 0], svf)
    bytes_of(v2.at[:, :, 0], sv3)
    bytes_of(evb.at[:, 0 : WIN * (nx - 1)], se)
    bytes_of(rb.at[0:15], sb)
    bytes_of(hz.at[:, 0 : 128 * (nz - 1)], sh)
    bytes_of(ws.at[0 : ny - 1], sw)
    bytes_of(rz.at[:, 0 : wy * (ny - 1)], sr)
    bytes_of(cs.at[0 : nz - 1], sc)
    bytes_of(rb.at[0:15], sd)
    give_c.wait()
    give_d.wait()


def per_device(topo, basis, blocks, counts, wpot, xc, occ, virt, eocc, evirt):
    nx, ny, nz = topo
    nbatch, points, columns = basis.shape
    rows, nocc = occ.shape
    wy = 4 * WIN // ny
    per = PER
    hbm = pl.BlockSpec(memory_space=pl.ANY)
    dma = pltpu.SemaphoreType.DMA
    scratch = [
        pltpu.SMEM((2, nbatch), jnp.int32),
        pltpu.SMEM((1, nbatch), jnp.int32),
        pltpu.VMEM(basis.shape, B16),
        pltpu.VMEM(wpot.shape, F32),
        pltpu.VMEM((1, nocc), F32),
        pltpu.VMEM(evirt.shape, F32),
        pltpu.VMEM((rows, nocc), F32),
        pltpu.VMEM((nbatch, points), F32),
        pltpu.VMEM((WIN, WIN), B16),
        pltpu.VMEM((WIN, nocc), B16),
        pltpu.VMEM((nocc, WIN), B16),
        pltpu.VMEM((nbatch // per, WIN, per * points), B16),
        pltpu.VMEM((WIN, WIN), F32),
        pltpu.VMEM((8, 2, SL, 128), HAM_LINK),
        pltpu.VMEM((16, SL, 128), HAM_LINK),
        pltpu.VMEM((SL, 128 * nz), B16),
        pltpu.VMEM((nx, nz, 2, BLK, WIN), B16),
        pltpu.VMEM((8, nx * WIN), F32),
        pltpu.VMEM((nocc, 128), F32),
        pltpu.VMEM((ny, SL, wy), VIRT_LINK),
        pltpu.VMEM((ny, SL, wy), VIRT_LINK),
        pltpu.VMEM((SL, nx * WIN), B16),
        pltpu.VMEM((nz, SL, 128), COEF_LINK),
        pltpu.VMEM((nz, SL, 128), COEF_LINK),
        pltpu.VMEM((2, 8, SL, 128), B16),
        dma((10,)),
        dma, dma((2,)),
        dma, dma((nz // 2 + 1,)),
        dma((2,)), dma((2, nz // 2 + 1)),
        dma, dma,
        dma, dma,
        dma, dma,
        dma, dma,
        dma, dma,
        dma, dma,
        dma, dma,
        dma, dma,
        dma, dma((2,)),
    ]
    coef, density = pl.pallas_call(
        functools.partial(kernel, topo),
        out_shape=(
            jax.ShapeDtypeStruct((rows, nocc), F32),
            jax.ShapeDtypeStruct((nbatch, points), F32),
        ),
        in_specs=[hbm] * 8,
        out_specs=(hbm, hbm),
        scratch_shapes=scratch,
        compiler_params=pltpu.CompilerParams(collective_id=0, has_side_effects=True),
        name="dfpt_cycle",
    )(basis, blocks.T, counts.reshape(1, -1), wpot, occ, virt, eocc.reshape(1, -1), evirt)
    live = lax.broadcasted_iota(jnp.int32, (nbatch, points), 1) < counts[:, None]
    return coef.astype(B16), jnp.where(live, xc * density, 0.0)


def solution(mesh):
    side = 1
    while 2 * side * side < mesh.shape["grid"]:
        side += 1
    topo = (mesh.shape["tile"], side, side)
    in_specs = (
        P(("grid", "tile"), None, None),
        P(("grid", "tile"), None),
        P(("grid", "tile")),
        P(("grid", "tile"), None),
        P(("grid", "tile"), None),
        P("grid", None),
        P("grid", "tile"),
        P(),
        P("tile"),
    )
    out_specs = (P("grid", None), P(("grid", "tile"), None))
    return jax.shard_map(
        functools.partial(per_device, topo),
        mesh=mesh, in_specs=in_specs, out_specs=out_specs, check_vma=False,
    )
```

```python
import functools

import jax
import jax.numpy as jnp
from jax import lax
from jax.experimental import pallas as pl
from jax.experimental.pallas import tpu as pltpu
from jax.sharding import PartitionSpec as P

MESH = pl.DeviceIdType.MESH
B16 = jnp.bfloat16
F32 = jnp.float32
HAM_LINK = jnp.bfloat16
VIRT_LINK = jnp.bfloat16
COEF_LINK = jnp.bfloat16
NT = (((1,), (1,)), ((), ()))
NN = (((1,), (0,)), ((), ()))
BLK = 64
WIN = 256
SL = 64
PER = 8
TALL = 192


def dot(a, b, dims=NN):
    return lax.dot_general(a, b, dims, preferred_element_type=F32)


def split(a):
    high = a.astype(B16)
    return high, (a - high.astype(F32)).astype(B16)


def kernel(
    topo, basis_in, blocks_in, counts_in, wpot_in, xc_in, occ, virt, eocc_in, evirt_in,
    coef_out, dens_out,
    blocks, counts, basis, wpot, xc, eocc, evirt, coef, dens, gmat,
    occw, occt, bw, mat, ps, po, rb, ro, hz, v2, evb, eot, ws, wr, rz, cs, cr, cw, cf, cp, staged,
    sl, sa, ra, sv1, rv1, sv2, rv2, svf, rvf, sv3, rv3, se, re,
    sb, rbs, sh, rh, sw, rw, sr, rr, sc, rc, sd, rd, ss, rs,
):
    nx, ny, nz = topo
    nq = ny * nz
    g = lax.axis_index("grid")
    t = lax.axis_index("tile")
    c = g % 2
    q = g // 2
    z = q % nz
    y = q // nz
    gother = (g + 2 * nq - 1 + 2 * c) % (2 * nq)
    qup = (q + 1) % nq
    qdown = (q + nq - 1) % nq
    qother = (q + nq - 1 + 2 * c) % nq
    s_me = t * 2 + c
    groups, _, span = bw.shape
    per = span // WIN
    nbatch = groups * per
    third = nbatch // 3

    def local(src, dst, sem):
        copy = pltpu.make_async_copy(src, dst, sem)
        copy.start()
        return copy

    def zring(d):
        zz = (z + d) % nz
        return zz, 2 * (y * nz + zz) + c

    def yring(d):
        yy = (y + d) % ny
        return yy, 2 * (yy * nz + z) + c

    def push(src, dst, send, recv, gg, tt):
        pltpu.make_async_remote_copy(
            src_ref=src, dst_ref=dst, send_sem=send, recv_sem=recv,
            device_id=(gg, tt), device_id_type=MESH,
        ).start()

    def bytes_of(ref, sem):
        pltpu.make_async_copy(ref, ref, sem).wait()

    def vstart(zz):
        return pl.multiple_of(WIN * zz - 128 * (zz // (nz - 1)), 128)

    def outward(n):
        return sorted(range(1, n), key=lambda d: (min(d, n - d), d))

    znear, ynear = outward(nz), outward(ny)
    zfar, yfar = znear[::-1], ynear[::-1]
    xnear = [0] + outward(nx)
    xfar = xnear[::-1]

    bar = pltpu.get_barrier_semaphore()
    own_chip = [(dc, dt) for dc in range(2) for dt in range(nx) if (dc, dt) != (0, 0)]
    for dc, dt in own_chip:
        pl.semaphore_signal(
            bar, inc=1, device_id=(2 * q + (c + dc) % 2, (t + dt) % nx), device_id_type=MESH
        )
    for qq in (qup, qdown):
        for cc in range(2):
            for tt in range(nx):
                pl.semaphore_signal(bar, inc=1, device_id=(2 * qq + cc, tt), device_id_type=MESH)
    for d in range(1, nz):
        pl.semaphore_signal(bar, inc=1, device_id=(zring(d)[1], t), device_id_type=MESH)
    for d in range(1, ny):
        pl.semaphore_signal(bar, inc=1, device_id=(yring(d)[1], t), device_id_type=MESH)

    own_rows = pl.ds(pl.multiple_of(BLK * c, BLK), BLK)
    far_rows = slice(2 * BLK, 3 * BLK)
    loads = [
        local(basis_in.at[pl.ds(third * k, third)], basis.at[pl.ds(third * k, third)], sl.at[k])
        for k in range(3)
    ]
    load_b = local(blocks_in, blocks, sl.at[8])
    load_n = local(counts_in, counts, sl.at[9])
    load_w = local(wpot_in, wpot, sl.at[3])
    load_v = local(virt.at[:, pl.ds(vstart(z), WIN)], v2.at[t, z, c], sl.at[4])

    pl.semaphore_wait(bar, len(own_chip) + 4 * nx + nz - 1 + ny - 1)

    sib = 2 * q + 1 - c
    push(occ, occw.at[far_rows], sa, ra.at[1], gother, t)
    push(occ, occw.at[own_rows], sa, ra.at[0], sib, t)
    right, left, across = (t + 1) % nx, (t + nx - 1) % nx, (t + 2) % nx
    steps = [[0], [1], [nz - 1]] + [znear[n : n + 2] for n in range(2, nz - 1, 2)]
    group_of = {d: n for n, ds in enumerate(steps) for d in ds}
    before = zring(nz - 1)
    chunk = virt.at[:, pl.ds(vstart(before[0]), WIN)]
    for k, to in enumerate((right, left)):
        push(chunk, staged.at[t], sv2.at[k], rv2.at[k, 1], g, to)
    for d in [1] + znear[2:] + [nz - 1]:
        zz, gg = zring(d)
        group = group_of[nz - d]
        push(virt.at[:, pl.ds(vstart(zz), WIN)], v2.at[t, z, c], sv1, rv1.at[group], gg, t)
    load_o = local(occ, occw.at[own_rows], sl.at[5])
    load_eo = local(eocc_in, eocc, sl.at[6])
    load_ev = local(evirt_in, evirt, sl.at[7])
    load_x = local(xc_in, xc, sl.at[10])
    mat[...] = jnp.zeros_like(mat)
    occw[3 * BLK : WIN, :] = jnp.zeros((BLK, occw.shape[1]), B16)

    row = lax.broadcasted_iota(jnp.int32, (TALL, 128), 0)
    col = lax.broadcasted_iota(jnp.int32, (TALL, 128), 1)
    lane = lax.broadcasted_iota(jnp.int32, (1, WIN), 1)
    load_w.wait()
    load_b.wait()
    load_n.wait()

    def integrate(n, carry):
        wides, scaled = [], []
        for j in range(per):
            b = per * n + j
            first = (BLK * (blocks[0, b] + c + 2)) % (3 * BLK)
            second = (BLK * (blocks[1, b] + c + 2)) % (3 * BLK)
            target = jnp.where(col < BLK, col + first, col - BLK + second)
            pick = jnp.where(row == target, 1.0, 0.0).astype(B16)
            spread = dot(pick, basis[b], NT)
            wide = spread.astype(B16)
            bw[n, :, WIN * j : WIN * j + WIN] = wide
            weight = jnp.where(lane < counts[0, b], wpot[pl.ds(b, 1), :], 0.0)
            wides.append(wide)
            scaled.append((spread * weight).astype(B16))
        mat[0:TALL, 0:TALL] += dot(jnp.concatenate(scaled, axis=1), jnp.concatenate(wides, axis=1), NT)
        return carry

    for k in range(3):
        loads[k].wait()
        lax.fori_loop(groups * k // 3, groups * (k + 1) // 3, integrate, 0)
        if k == 0:
            load_v.wait()
            for n, to in enumerate((right, left)):
                push(v2.at[t, z, c], v2.at[t, z, c], sv2.at[n], rv2.at[n, 0], g, to)

    load_o.wait()
    bytes_of(occw.at[pl.ds(pl.multiple_of(BLK * (1 - c), BLK), BLK)], ra.at[0])
    bytes_of(occw.at[far_rows], ra.at[1])
    occt[...] = jnp.transpose(occw[...].astype(F32)).astype(B16)
    high, low = split(mat[...])
    part = dot(occt[...], high) + dot(occt[...], low)
    half_lane = lax.broadcasted_iota(jnp.int32, (SL // 2, 128), 1) < BLK
    for s in range(2 * nx):
        rows = part[SL * s : SL * s + SL]
        ps[s] = rows[:, 0:128].astype(HAM_LINK)
        top, bottom = rows[0 : SL // 2, 128:256], rows[SL // 2 : SL, 128:256]
        po[s] = jnp.where(half_lane, top, pltpu.roll(bottom, BLK, 1)).astype(HAM_LINK)


    def along_x(n):
        ds = steps[n]
        bytes_of(v2.at[t, 0 : len(ds), c], rv1.at[n])
        for d in ds:
            mine = v2.at[t, (z + d) % nz, c]
            push(mine, mine, sv2.at[0], rv2.at[0, n], g, right)
            push(mine, mine, sv2.at[1], rv2.at[1, n], g, left)

    slot = 4 * c + t
    rb[slot] = ps[s_me]

    def give_ham():
        for dt in xfar:
            tt = (t + dt) % nx
            for cc in range(2):
                push(po.at[tt * 2 + cc], ro.at[slot], sb.at[1], rbs.at[1], 2 * qother + cc, tt)
            for dc in range(2):
                if dc or dt:
                    cc = (c + dc) % 2
                    push(ps.at[tt * 2 + cc], rb.at[slot], sb.at[0], rbs.at[0], 2 * q + cc, tt)

    give_ham()
    for k, (frm, to) in enumerate(((left, right), (right, left))):
        bytes_of(staged.at[0], rv2.at[k, 1])
        if k == 1:
            push(staged.at[frm], staged.at[frm], svf, rvf.at[0], g, to)
        push(staged.at[frm], v2.at[frm, z, c], ss, rs.at[k], before[1], t)
    for n in range(2, len(steps) - 1):
        along_x(n)
    bytes_of(staged.at[0], rvf.at[0])
    push(staged.at[across], v2.at[across, z, c], ss, rs.at[2], before[1], t)
    load_eo.wait()
    load_x.wait()
    load_ev.wait()
    eot[...] = jnp.transpose(jnp.broadcast_to(eocc[...], (128, eocc.shape[1])))
    evb[:, pl.ds(pl.multiple_of(WIN * t, WIN), WIN)] = jnp.broadcast_to(
        evirt[pl.ds(vstart(z), WIN)].reshape(1, WIN), (8, WIN)
    )
    mine_e = evb.at[:, pl.ds(pl.multiple_of(WIN * t, WIN), WIN)]
    for d in range(1, nx):
        push(mine_e, mine_e, se, re, g, (t + d) % nx)

    bytes_of(rb.at[0:7], rbs.at[0])
    bytes_of(ro, rbs.at[1])
    ham = rb[0].astype(F32)
    for k in range(1, 8):
        ham = ham + rb[k].astype(F32)
    above = ro[0].astype(F32)
    below = ro[4].astype(F32)
    for k in range(1, 4):
        above = above + ro[k].astype(F32)
        below = below + ro[4 + k].astype(F32)
    halo = jnp.concatenate([
        jnp.where(half_lane, below, pltpu.roll(above, BLK, 1)),
        jnp.where(half_lane, pltpu.roll(below, BLK, 1), above),
    ], axis=0)
    ham = ham + halo
    zcols = lambda zz: pl.ds(pl.multiple_of(128 * zz, 128), 128)
    hz[:, zcols(z)] = ham.astype(B16)
    for d in zfar:
        push(hz.at[:, zcols(z)], hz.at[:, zcols(z)], sh, rh, zring(d)[1], t)
    along_x(len(steps) - 1)
    bytes_of(v2.at[t, 0, c], rv1.at[1])
    push(v2.at[t, :, c], v2.at[t, :, c], sv3, rv3.at[0], sib, t)

    def to_sibling(tt, n, ds):
        for d in ds:
            block = v2.at[tt, (z + d) % nz, c]
            push(block, block, sv3, rv3.at[n], sib, t)

    rightward = (0, nz - 2)
    for n, ds in enumerate(steps):
        if n == 1:
            continue
        for k, (frm, to) in enumerate(((left, right), (right, left))):
            bytes_of(v2.at[frm, 0 : len(ds), c], rv2.at[k, n])
            for d in ds:
                if (d in rightward) == (k == 0):
                    theirs = v2.at[frm, (z + d) % nz, c]
                    push(theirs, theirs, svf, rvf.at[2 if n == len(steps) - 1 else 1], g, to)
            to_sibling(frm, 1 + k, ds)
    for k, frm in enumerate((left, right)):
        bytes_of(v2.at[frm, 0, c], rs.at[k])
        to_sibling(frm, 1 + k, [1])
    bytes_of(hz.at[:, 0 : 128 * (nz - 1)], rh)

    share = 8 // ny

    def virtual(tt, n):
        bytes_of(v2.at[tt, :, 1 - c], rv3.at[n])
        part = dot(hz[...], v2[tt].reshape(nz * 128, WIN))
        for k in range(8):
            i, a = 16 * (k // 2), 128 * (k % 2)
            ws[n, k] = part[i : i + 16, a : a + 128].astype(VIRT_LINK)
        wr[n, y] = ws[n, pl.ds(y * share, share)]
        for d in yfar:
            yy, gg = yring(d)
            push(ws.at[n, pl.ds(yy * share, share)], wr.at[n, y], sw, rw.at[n], gg, t)

    def rotate(tt, n):
        bytes_of(wr.at[n, 0 : ny - 1], rw.at[n])
        for h in range(share):
            k = y * share + h
            total = wr[n, 0, h].astype(F32)
            for yy in range(1, ny):
                total = total + wr[n, yy, h].astype(F32)
            i = pl.multiple_of(SL * s_me + 16 * (k // 2), 16)
            a = pl.multiple_of(WIN * tt + 128 * (k % 2), 128)
            gap = eot[pl.ds(i, 16), 0:1] - evb[0:1, pl.ds(a, 128)]
            repeat = lax.broadcasted_iota(jnp.int32, (16, 128), 1) * 0 + k % 2 < z // (nz - 1)
            rz[n, k] = jnp.where(repeat, 0.0, total / gap).astype(B16)
        mine = rz.at[n, pl.ds(y * share, share)]
        for d in yfar:
            push(mine, mine, sr, rr.at[n], yring(d)[1], t)

    def respond_to(tt, n):
        bytes_of(rz.at[n, 0 : (ny - 1) * share], rr.at[n])
        turn = jnp.concatenate([
            jnp.concatenate([rz[n, k], rz[n, k + 1]], axis=1) for k in range(0, 8, 2)
        ], axis=0)
        return dot(turn, v2[tt].reshape(nz * 128, WIN), NT)

    virtual(t, 0)
    last = steps[-1]
    bytes_of(v2.at[across, 0, c], rs.at[2])
    bytes_of(v2.at[across, 0 : nz - 1 - len(last), c], rvf.at[1])
    to_sibling(across, 3, [d for d in range(nz) if d not in last])
    virtual(left, 1)
    bytes_of(v2.at[across, 0 : len(last), c], rvf.at[2])
    to_sibling(across, 3, last)
    virtual(right, 2)
    virtual(across, 3)
    bytes_of(evb.at[:, 0 : WIN * (nx - 1)], re)
    tiles = (t, left, right, across)
    for n in range(nx - 1):
        rotate(tiles[n], n)
    rotate(tiles[nx - 1], nx - 1)
    part = respond_to(tiles[0], 0)
    for n in range(1, nx - 1):
        part += respond_to(tiles[n], n)
    part += respond_to(tiles[nx - 1], nx - 1)
    for k in range(nz):
        cs[k] = part[:, 128 * k : 128 * k + 128].astype(COEF_LINK)
    cr[z] = cs[z]
    for d in zfar:
        zz, gg = zring(d)
        push(cs.at[zz], cr.at[z], sc, rc, gg, t)
    bytes_of(cr.at[0 : nz - 1], rc)
    done = cr[0].astype(F32)
    for k in range(1, nz):
        done = done + cr[k].astype(F32)
    cw[s_me] = done.astype(B16)
    top, bottom = done[0 : SL // 2], done[SL // 2 : SL]
    cp[0] = jnp.where(half_lane, pltpu.roll(top, BLK, 1), bottom).astype(B16)
    cp[1] = jnp.where(half_lane, top, pltpu.roll(bottom, BLK, 1)).astype(B16)

    for dt in xfar:
        tt = (t + dt) % nx
        push(cp.at[0], cf.at[s_me], sd.at[1], rd.at[1], 2 * qup, tt)
        push(cp.at[1], cf.at[s_me], sd.at[1], rd.at[1], 2 * qdown + 1, tt)
        for dc in range(2):
            if dc or dt:
                push(cw.at[s_me], cw.at[s_me], sd.at[0], rd.at[0], 2 * q + (c + dc) % 2, tt)
    bytes_of(cw.at[0:7], rd.at[0])
    near = cw[...].reshape(8 * SL, 128)
    krow = lax.broadcasted_iota(jnp.int32, (BLK, 128), 0)
    kcol = lax.broadcasted_iota(jnp.int32, (BLK, 128), 1)
    pick = jnp.where(kcol == krow + BLK * c, 1.0, 0.0).astype(B16)
    coef[...] = dot(pick, near, NT).astype(B16)
    give_c = local(coef, coef_out, sl.at[0])
    gmat[:, 0:128] = dot(occw[...], near).astype(B16)
    bytes_of(cf, rd.at[1])
    pieces = []
    for k in range(8):
        packed = cf[k]
        pieces += [packed, pltpu.roll(packed.astype(F32), BLK, 1).astype(B16)]
    far = jnp.concatenate(pieces, axis=0)
    gmat[:, 128:256] = dot(occw[...], far).astype(B16)

    def respond(n, carry):
        wide = bw[n]
        resp = dot(gmat[0:TALL, 0:TALL], wide)
        total = jnp.sum(resp * wide.astype(F32), axis=0, keepdims=True)
        for j in range(per):
            b = per * n + j
            value = xc[pl.ds(b, 1), :] * (4.0 * total[:, WIN * j : WIN * j + WIN])
            dens[pl.ds(b, 1), :] = jnp.where(lane < counts[0, b], value, 0.0)
        return carry

    lax.fori_loop(0, groups, respond, 0)
    give_d = local(dens, dens_out, sl.at[1])
    bytes_of(occw.at[0:128], sa)
    bytes_of(v2.at[0, 0 : nz - 1, 0], sv1)
    bytes_of(v2.at[0, :, 0], sv2.at[0])
    bytes_of(v2.at[0, :, 0], sv2.at[1])
    bytes_of(v2.at[0, :, 0], svf)
    bytes_of(v2.at[0:3, 0, 0], ss)
    bytes_of(v2.at[:, :, 0], sv3)
    bytes_of(evb.at[:, 0 : WIN * (nx - 1)], se)
    bytes_of(rb.at[0:7], sb.at[0])
    bytes_of(ro, sb.at[1])
    bytes_of(hz.at[:, 0 : 128 * (nz - 1)], sh)
    bytes_of(wr.at[:, 0 : ny - 1], sw)
    bytes_of(rz.at[:, 0 : (ny - 1) * share], sr)
    bytes_of(cs.at[0 : nz - 1], sc)
    bytes_of(cw.at[0:7], sd.at[0])
    bytes_of(cf, sd.at[1])
    give_c.wait()
    give_d.wait()


def per_device(topo, basis, blocks, counts, wpot, xc, occ, virt, eocc, evirt):
    nx, ny, nz = topo
    nbatch, points, columns = basis.shape
    rows, nocc = occ.shape
    per = PER
    anywhere = pl.BlockSpec(memory_space=pl.ANY)
    dma = pltpu.SemaphoreType.DMA
    scratch = [
        pltpu.SMEM((2, nbatch), jnp.int32),
        pltpu.SMEM((1, nbatch), jnp.int32),
        pltpu.VMEM(basis.shape, B16),
        pltpu.VMEM(wpot.shape, F32),
        pltpu.VMEM(xc.shape, F32),
        pltpu.VMEM((1, nocc), F32),
        pltpu.VMEM(evirt.shape, F32),
        pltpu.VMEM((rows, nocc), B16),
        pltpu.VMEM((nbatch, points), F32),
        pltpu.VMEM((WIN, WIN), B16),
        pltpu.VMEM((WIN, nocc), B16),
        pltpu.VMEM((nocc, WIN), B16),
        pltpu.VMEM((nbatch // per, TALL, per * points), B16),
        pltpu.VMEM((WIN, WIN), F32),
        pltpu.VMEM((8, SL, 128), HAM_LINK),
        pltpu.VMEM((8, SL // 2, 128), HAM_LINK),
        pltpu.VMEM((8, SL, 128), HAM_LINK),
        pltpu.VMEM((8, SL // 2, 128), HAM_LINK),
        pltpu.VMEM((SL, 128 * nz), B16),
        pltpu.VMEM((nx, nz, 2, BLK, WIN), B16),
        pltpu.VMEM((8, nx * WIN), F32),
        pltpu.VMEM((nocc, 128), F32),
        pltpu.VMEM((nx, 8, 16, 128), VIRT_LINK),
        pltpu.VMEM((nx, ny, 8 // ny, 16, 128), VIRT_LINK),
        pltpu.VMEM((nx, 8, 16, 128), B16),
        pltpu.VMEM((nz, SL, 128), COEF_LINK),
        pltpu.VMEM((nz, SL, 128), COEF_LINK),
        pltpu.VMEM((8, SL, 128), B16),
        pltpu.VMEM((8, SL // 2, 128), B16),
        pltpu.VMEM((2, SL // 2, 128), B16),
        pltpu.VMEM((nx, BLK, WIN), B16),
        dma((11,)),
        dma, dma((2,)),
        dma, dma((nz // 2 + 2,)),
        dma((2,)), dma((2, nz // 2 + 2)),
        dma, dma((3,)),
        dma, dma((4,)),
        dma, dma,
        dma((2,)), dma((2,)),
        dma, dma,
        dma, dma((4,)),
        dma, dma((4,)),
        dma, dma,
        dma((2,)), dma((2,)),
        dma, dma((3,)),
    ]
    coef, potential = pl.pallas_call(
        functools.partial(kernel, topo),
        out_shape=(
            jax.ShapeDtypeStruct((rows, nocc), B16),
            jax.ShapeDtypeStruct((nbatch, points), F32),
        ),
        in_specs=[pl.BlockSpec(memory_space=pltpu.HBM)] * 9,
        out_specs=(anywhere, anywhere),
        scratch_shapes=scratch,
        compiler_params=pltpu.CompilerParams(collective_id=0, has_side_effects=True, vmem_limit_bytes=24 << 20),
        name="dfpt_cycle",
    )(*(
        pltpu.with_memory_space_constraint(array, pltpu.HBM)
        for array in (
            basis, blocks.T, counts.reshape(1, -1), wpot, xc, occ, virt,
            eocc.reshape(1, -1), evirt,
        )
    ))
    return pl.pallas_call(
        hand_out,
        out_shape=(
            jax.ShapeDtypeStruct(coef.shape, coef.dtype),
            jax.ShapeDtypeStruct(potential.shape, potential.dtype),
        ),
        in_specs=[anywhere] * 2,
        out_specs=(anywhere, anywhere),
        scratch_shapes=[dma((2,))],
        compiler_params=pltpu.CompilerParams(vmem_limit_bytes=1 << 20),
        name="hand_out",
    )(coef, potential)


def hand_out(coef, potential, coef_out, potential_out, sems):
    first = pltpu.make_async_copy(coef, coef_out, sems.at[0])
    second = pltpu.make_async_copy(potential, potential_out, sems.at[1])
    first.start()
    second.start()
    first.wait()
    second.wait()


def solution(mesh):
    side = 1
    while 2 * side * side < mesh.shape["grid"]:
        side += 1
    topo = (mesh.shape["tile"], side, side)
    in_specs = (
        P(("grid", "tile"), None, None),
        P(("grid", "tile"), None),
        P(("grid", "tile")),
        P(("grid", "tile"), None),
        P(("grid", "tile"), None),
        P("grid", None),
        P("grid", "tile"),
        P(),
        P("tile"),
    )
    out_specs = (P("grid", None), P(("grid", "tile"), None))
    return jax.shard_map(
        functools.partial(per_device, topo),
        mesh=mesh, in_specs=in_specs, out_specs=out_specs, check_vma=False,
    )
```

```python
import functools

import jax
import jax.numpy as jnp
from jax import lax
from jax.experimental import pallas as pl
from jax.experimental.pallas import tpu as pltpu
from jax.sharding import PartitionSpec as P

MESH = pl.DeviceIdType.MESH
B16 = jnp.bfloat16
F32 = jnp.float32
HAM_LINK = jnp.bfloat16
VIRT_LINK = jnp.bfloat16
COEF_LINK = jnp.bfloat16
NT = (((1,), (1,)), ((), ()))
NN = (((1,), (0,)), ((), ()))
BLK = 64
WIN = 256
SL = 64
PER = 8
HALVES = 1
TALL = 192


def dot(a, b, dims=NN):
    return lax.dot_general(a, b, dims, preferred_element_type=F32)


def split(a):
    high = a.astype(B16)
    return high, (a - high.astype(F32)).astype(B16)


def kernel(
    topo, basis_in, blocks_in, counts_in, wpot_in, xc_in, occ, virt_in, eocc_in, evirt_in,
    coef_out, dens_out,
    blocks, counts, basis, wpot, xc, eocc, evirt, coef, dens, gmat,
    occw, occt, bw, mat, ps, po, rb, ro, hz, v2, evb, eot, ws, wr, rz, cs, cr, cw, cf, cp, staged, virt,
    sl, sa, ra, sv1, rv1, sv2, rv2, svf, rvf, sv3, rv3, se, re,
    sb, rbs, sh, rh, sw, rw, sr, rr, sc, rc, sd, rd, ss, rs,
):
    nx, ny, nz = topo
    nq = ny * nz
    g = lax.axis_index("grid")
    t = lax.axis_index("tile")
    c = g % 2
    q = g // 2
    z = q % nz
    y = q // nz
    gother = (g + 2 * nq - 1 + 2 * c) % (2 * nq)
    qup = (q + 1) % nq
    qdown = (q + nq - 1) % nq
    qother = (q + nq - 1 + 2 * c) % nq
    s_me = t * 2 + c
    groups, _, span = bw.shape
    per = span // WIN
    nbatch = groups * per
    third = nbatch // 3

    def local(src, dst, sem):
        copy = pltpu.make_async_copy(src, dst, sem)
        copy.start()
        return copy

    def zring(d):
        zz = (z + d) % nz
        return zz, 2 * (y * nz + zz) + c

    def yring(d):
        yy = (y + d) % ny
        return yy, 2 * (yy * nz + z) + c

    def push(src, dst, send, recv, gg, tt):
        pltpu.make_async_remote_copy(
            src_ref=src, dst_ref=dst, send_sem=send, recv_sem=recv,
            device_id=(gg, tt), device_id_type=MESH,
        ).start()

    def bytes_of(ref, sem):
        pltpu.make_async_copy(ref, ref, sem).wait()

    def vstart(zz):
        return pl.multiple_of(WIN * zz - 128 * (zz // (nz - 1)), 128)

    def outward(n):
        return sorted(range(1, n), key=lambda d: (min(d, n - d), d))

    znear, ynear = outward(nz), outward(ny)
    zfar, yfar = znear[::-1], ynear[::-1]
    xnear = [0] + outward(nx)
    xfar = xnear[::-1]

    bar = pltpu.get_barrier_semaphore()
    own_chip = [(dc, dt) for dc in range(2) for dt in range(nx) if (dc, dt) != (0, 0)]
    for dc, dt in own_chip:
        pl.semaphore_signal(
            bar, inc=1, device_id=(2 * q + (c + dc) % 2, (t + dt) % nx), device_id_type=MESH
        )
    for qq in (qup, qdown):
        for cc in range(2):
            for tt in range(nx):
                pl.semaphore_signal(bar, inc=1, device_id=(2 * qq + cc, tt), device_id_type=MESH)
    for d in range(1, nz):
        pl.semaphore_signal(bar, inc=1, device_id=(zring(d)[1], t), device_id_type=MESH)
    for d in range(1, ny):
        pl.semaphore_signal(bar, inc=1, device_id=(yring(d)[1], t), device_id_type=MESH)

    own_rows = pl.ds(pl.multiple_of(BLK * c, BLK), BLK)
    far_rows = slice(2 * BLK, 3 * BLK)
    load_o = local(occ, occw.at[own_rows], sl.at[5])
    load_u = local(virt_in, virt, sl.at[11])
    loads = [
        local(basis_in.at[pl.ds(third * k, third)], basis.at[pl.ds(third * k, third)], sl.at[k])
        for k in range(3)
    ]
    load_b = local(blocks_in, blocks, sl.at[8])
    load_n = local(counts_in, counts, sl.at[9])
    load_w = local(wpot_in, wpot, sl.at[3])
    load_v = local(virt_in.at[:, pl.ds(vstart(z), WIN)], v2.at[t, z, c], sl.at[4])

    pl.semaphore_wait(bar, len(own_chip) + 4 * nx + nz - 1 + ny - 1)

    sib = 2 * q + 1 - c
    load_o.wait()
    push(occw.at[own_rows], occw.at[far_rows], sa, ra.at[1], gother, t)
    push(occw.at[own_rows], occw.at[own_rows], sa, ra.at[0], sib, t)
    load_u.wait()
    right, left, across = (t + 1) % nx, (t + nx - 1) % nx, (t + 2) % nx
    steps = [[0], [1], [nz - 1]] + [znear[n : n + 2] for n in range(2, nz - 1, 2)]
    group_of = {d: n for n, ds in enumerate(steps) for d in ds}
    before = zring(nz - 1)
    chunk = virt.at[:, pl.ds(vstart(before[0]), WIN)]
    for k, to in enumerate((right, left)):
        push(chunk, staged.at[t], sv2.at[k], rv2.at[k, 1], g, to)
    for d in [nz // 2, 1] + znear[2:-1] + [nz - 1]:
        zz, gg = zring(d)
        group = group_of[nz - d]
        push(virt.at[:, pl.ds(vstart(zz), WIN)], v2.at[t, z, c], sv1, rv1.at[group], gg, t)
    load_eo = local(eocc_in, eocc, sl.at[6])
    load_ev = local(evirt_in, evirt, sl.at[7])
    load_x = local(xc_in, xc, sl.at[10])
    mat[...] = jnp.zeros_like(mat)
    occw[3 * BLK : WIN, :] = jnp.zeros((BLK, occw.shape[1]), B16)

    row = lax.broadcasted_iota(jnp.int32, (TALL, 128), 0)
    col = lax.broadcasted_iota(jnp.int32, (TALL, 128), 1)
    lane = lax.broadcasted_iota(jnp.int32, (1, WIN), 1)
    load_w.wait()
    load_b.wait()
    load_n.wait()

    def integrate(n, carry):
        wides, scaled = [], []
        for j in range(per):
            b = per * n + j
            first = (BLK * (blocks[0, b] + c + 2)) % (3 * BLK)
            second = (BLK * (blocks[1, b] + c + 2)) % (3 * BLK)
            target = jnp.where(col < BLK, col + first, col - BLK + second)
            pick = jnp.where(row == target, 1.0, 0.0).astype(B16)
            spread = dot(pick, basis[b], NT)
            wide = spread.astype(B16)
            bw[n, :, WIN * j : WIN * j + WIN] = wide
            weight = jnp.where(lane < counts[0, b], wpot[pl.ds(b, 1), :], 0.0)
            wides.append(wide)
            scaled.append((spread * weight).astype(B16))
        mat[0:TALL, 0:TALL] += dot(jnp.concatenate(scaled, axis=1), jnp.concatenate(wides, axis=1), NT)
        return carry

    for k in range(3):
        loads[k].wait()
        lax.fori_loop(groups * k // 3, groups * (k + 1) // 3, integrate, 0)
        if k == 0:
            load_v.wait()
            for n, to in enumerate((right, left)):
                push(v2.at[t, z, c], v2.at[t, z, c], sv2.at[n], rv2.at[n, 0], g, to)

    bytes_of(occw.at[pl.ds(pl.multiple_of(BLK * (1 - c), BLK), BLK)], ra.at[0])
    bytes_of(occw.at[far_rows], ra.at[1])
    occt[...] = jnp.transpose(occw[...].astype(F32)).astype(B16)
    high, low = split(mat[...])
    part = dot(occt[...], high) + dot(occt[...], low)
    half_lane = lax.broadcasted_iota(jnp.int32, (SL // 2, 128), 1) < BLK
    for s in range(2 * nx):
        rows = part[SL * s : SL * s + SL]
        ps[s] = rows[:, 0:128].astype(HAM_LINK)
        top, bottom = rows[0 : SL // 2, 128:256], rows[SL // 2 : SL, 128:256]
        po[s] = jnp.where(half_lane, top, pltpu.roll(bottom, BLK, 1)).astype(HAM_LINK)


    def along_x(n):
        ds = steps[n]
        bytes_of(v2.at[t, 0 : len(ds), c], rv1.at[n])
        for d in ds:
            mine = v2.at[t, (z + d) % nz, c]
            push(mine, mine, sv2.at[0], rv2.at[0, n], g, right)
            push(mine, mine, sv2.at[1], rv2.at[1, n], g, left)

    slot = 4 * c + t
    rb[slot] = ps[s_me]

    def give_ham():
        for dt in xfar:
            tt = (t + dt) % nx
            for cc in range(2):
                push(po.at[tt * 2 + cc], ro.at[slot], sb.at[1], rbs.at[1], 2 * qother + cc, tt)
            for dc in range(2):
                if dc or dt:
                    cc = (c + dc) % 2
                    push(ps.at[tt * 2 + cc], rb.at[slot], sb.at[0], rbs.at[0], 2 * q + cc, tt)

    give_ham()
    for k, (frm, to) in enumerate(((left, right), (right, left))):
        bytes_of(staged.at[0], rv2.at[k, 1])
        if k == 1:
            push(staged.at[frm], staged.at[frm], svf, rvf.at[0], g, to)
        push(staged.at[frm], v2.at[frm, z, c], ss, rs.at[k], before[1], t)
    for n in range(2, len(steps)):
        along_x(n)
    bytes_of(staged.at[0], rvf.at[0])
    push(staged.at[across], v2.at[across, z, c], ss, rs.at[2], before[1], t)
    load_eo.wait()
    load_x.wait()
    load_ev.wait()
    eot[...] = jnp.transpose(jnp.broadcast_to(eocc[...], (128, eocc.shape[1])))
    evb[:, pl.ds(pl.multiple_of(WIN * t, WIN), WIN)] = jnp.broadcast_to(
        evirt[pl.ds(vstart(z), WIN)].reshape(1, WIN), (8, WIN)
    )
    mine_e = evb.at[:, pl.ds(pl.multiple_of(WIN * t, WIN), WIN)]
    for d in range(1, nx):
        push(mine_e, mine_e, se, re, g, (t + d) % nx)

    bytes_of(rb.at[0:7], rbs.at[0])
    bytes_of(ro, rbs.at[1])
    ham = rb[0].astype(F32)
    for k in range(1, 8):
        ham = ham + rb[k].astype(F32)
    above = ro[0].astype(F32)
    below = ro[4].astype(F32)
    for k in range(1, 4):
        above = above + ro[k].astype(F32)
        below = below + ro[4 + k].astype(F32)
    halo = jnp.concatenate([
        jnp.where(half_lane, below, pltpu.roll(above, BLK, 1)),
        jnp.where(half_lane, pltpu.roll(below, BLK, 1), above),
    ], axis=0)
    ham = ham + halo
    zcols = lambda zz: pl.ds(pl.multiple_of(128 * zz, 128), 128)
    hz[:, zcols(z)] = ham.astype(B16)
    for d in zfar:
        push(hz.at[:, zcols(z)], hz.at[:, zcols(z)], sh, rh, zring(d)[1], t)
    bytes_of(v2.at[t, 0, c], rv1.at[1])
    push(v2.at[t, :, c], v2.at[t, :, c], sv3, rv3.at[0], sib, t)

    def to_sibling(tt, n, ds):
        for d in ds:
            block = v2.at[tt, (z + d) % nz, c]
            push(block, block, sv3, rv3.at[n], sib, t)

    rightward = (0, nz - 2)
    for n, ds in enumerate(steps):
        if n == 1:
            continue
        for k, (frm, to) in enumerate(((left, right), (right, left))):
            bytes_of(v2.at[frm, 0 : len(ds), c], rv2.at[k, n])
            for d in ds:
                if (d in rightward) == (k == 0):
                    theirs = v2.at[frm, (z + d) % nz, c]
                    push(theirs, theirs, svf, rvf.at[2 if n == len(steps) - 1 else 1], g, to)
            to_sibling(frm, 1 + k, ds)
    for k, frm in enumerate((left, right)):
        bytes_of(v2.at[frm, 0, c], rs.at[k])
        to_sibling(frm, 1 + k, [1])
    bytes_of(hz.at[:, 0 : 128 * (nz - 1)], rh)

    share = 8 // ny

    def virtual(tt, n):
        bytes_of(v2.at[tt, :, 1 - c], rv3.at[n])
        part = dot(hz[...], v2[tt].reshape(nz * 128, WIN))
        for k in range(8):
            i, a = 16 * (k // 2), 128 * (k % 2)
            ws[n, k] = part[i : i + 16, a : a + 128].astype(VIRT_LINK)
        wr[n, y] = ws[n, pl.ds(y * share, share)]
        for d in yfar:
            yy, gg = yring(d)
            push(ws.at[n, pl.ds(yy * share, share)], wr.at[n, y], sw, rw.at[n], gg, t)

    def rotate(tt, n):
        bytes_of(wr.at[n, 0 : ny - 1], rw.at[n])
        for h in range(share):
            k = y * share + h
            total = wr[n, 0, h].astype(F32)
            for yy in range(1, ny):
                total = total + wr[n, yy, h].astype(F32)
            i = pl.multiple_of(SL * s_me + 16 * (k // 2), 16)
            a = pl.multiple_of(WIN * tt + 128 * (k % 2), 128)
            gap = eot[pl.ds(i, 16), 0:1] - evb[0:1, pl.ds(a, 128)]
            repeat = lax.broadcasted_iota(jnp.int32, (16, 128), 1) * 0 + k % 2 < z // (nz - 1)
            rz[n, k] = jnp.where(repeat, 0.0, total / gap).astype(B16)
        mine = rz.at[n, pl.ds(y * share, share)]
        for d in yfar:
            push(mine, mine, sr, rr.at[n], yring(d)[1], t)

    def respond_to(tt, n):
        bytes_of(rz.at[n, 0 : (ny - 1) * share], rr.at[n])
        turn = jnp.concatenate([
            jnp.concatenate([rz[n, k], rz[n, k + 1]], axis=1) for k in range(0, 8, 2)
        ], axis=0)
        return dot(turn, v2[tt].reshape(nz * 128, WIN), NT)

    virtual(t, 0)
    last = steps[-1]
    bytes_of(v2.at[across, 0, c], rs.at[2])
    bytes_of(v2.at[across, 0 : nz - 1 - len(last), c], rvf.at[1])
    to_sibling(across, 3, [d for d in range(nz) if d not in last])
    virtual(left, 1)
    bytes_of(v2.at[across, 0 : len(last), c], rvf.at[2])
    to_sibling(across, 3, last)
    virtual(right, 2)
    virtual(across, 3)
    bytes_of(evb.at[:, 0 : WIN * (nx - 1)], re)
    tiles = (t, left, right, across)
    for n in range(nx - 1):
        rotate(tiles[n], n)
    rotate(tiles[nx - 1], nx - 1)
    part = respond_to(tiles[0], 0)
    for n in range(1, nx - 1):
        part += respond_to(tiles[n], n)
    part += respond_to(tiles[nx - 1], nx - 1)
    rise = SL // HALVES
    for h in range(HALVES):
        for k in range(nz):
            cs[h, k] = part[rise * h : rise * (h + 1), 128 * k : 128 * k + 128].astype(COEF_LINK)
    for h in range(HALVES):
        for d in zfar:
            zz, gg = zring(d)
            push(cs.at[h, zz], cr.at[h, z], sc, rc.at[h], gg, t)
    quarter_lane = lax.broadcasted_iota(jnp.int32, (rise // 2, 128), 1) < BLK
    for h in range(HALVES):
        cr[h, z] = cs[h, z]
        bytes_of(cr.at[h, 0 : nz - 1], rc.at[h])
        done = cr[h, 0].astype(F32)
        for k in range(1, nz):
            done = done + cr[h, k].astype(F32)
        cw[s_me, h] = done.astype(B16)
        top, bottom = done[0 : rise // 2], done[rise // 2 : rise]
        cp[0, h] = jnp.where(quarter_lane, pltpu.roll(top, BLK, 1), bottom).astype(B16)
        cp[1, h] = jnp.where(quarter_lane, top, pltpu.roll(bottom, BLK, 1)).astype(B16)
        for dt in xfar:
            tt = (t + dt) % nx
            push(cp.at[0, h], cf.at[s_me, h], sd.at[1], rd.at[1], 2 * qup, tt)
            push(cp.at[1, h], cf.at[s_me, h], sd.at[1], rd.at[1], 2 * qdown + 1, tt)
            for dc in range(2):
                if dc or dt:
                    mine = cw.at[s_me, h]
                    push(mine, mine, sd.at[0], rd.at[0], 2 * q + (c + dc) % 2, tt)
    bytes_of(cw.at[0:7], rd.at[0])
    near = cw[...].reshape(8 * SL, 128)
    krow = lax.broadcasted_iota(jnp.int32, (BLK, 128), 0)
    kcol = lax.broadcasted_iota(jnp.int32, (BLK, 128), 1)
    pick = jnp.where(kcol == krow + BLK * c, 1.0, 0.0).astype(B16)
    coef[...] = dot(pick, near, NT).astype(B16)
    give_c = local(coef, coef_out, sl.at[0])
    gmat[:, 0:128] = dot(occw[...], near).astype(B16)
    bytes_of(cf, rd.at[1])
    pieces = []
    for k in range(8):
        for h in range(HALVES):
            packed = cf[k, h]
            pieces += [packed, pltpu.roll(packed.astype(F32), BLK, 1).astype(B16)]
    far = jnp.concatenate(pieces, axis=0)
    gmat[:, 128:256] = dot(occw[...], far).astype(B16)

    def respond(n, carry):
        wide = bw[n]
        resp = dot(gmat[0:TALL, 0:TALL], wide)
        total = jnp.sum(resp * wide.astype(F32), axis=0, keepdims=True)
        for j in range(per):
            b = per * n + j
            value = xc[pl.ds(b, 1), :] * (4.0 * total[:, WIN * j : WIN * j + WIN])
            dens[pl.ds(b, 1), :] = jnp.where(lane < counts[0, b], value, 0.0)
        return carry

    lax.fori_loop(0, groups, respond, 0)
    give_d = local(dens, dens_out, sl.at[1])
    bytes_of(occw.at[0:128], sa)
    bytes_of(v2.at[0, 0 : nz - 1, 0], sv1)
    bytes_of(v2.at[0, :, 0], sv2.at[0])
    bytes_of(v2.at[0, :, 0], sv2.at[1])
    bytes_of(v2.at[0, :, 0], svf)
    bytes_of(v2.at[0:3, 0, 0], ss)
    bytes_of(v2.at[:, :, 0], sv3)
    bytes_of(evb.at[:, 0 : WIN * (nx - 1)], se)
    bytes_of(rb.at[0:7], sb.at[0])
    bytes_of(ro, sb.at[1])
    bytes_of(hz.at[:, 0 : 128 * (nz - 1)], sh)
    bytes_of(wr.at[:, 0 : ny - 1], sw)
    bytes_of(rz.at[:, 0 : (ny - 1) * share], sr)
    bytes_of(cs.at[:, 0 : nz - 1], sc)
    bytes_of(cw.at[0:7], sd.at[0])
    bytes_of(cf, sd.at[1])
    give_c.wait()
    give_d.wait()


def per_device(topo, basis, blocks, counts, wpot, xc, occ, virt, eocc, evirt):
    nx, ny, nz = topo
    nbatch, points, columns = basis.shape
    rows, nocc = occ.shape
    per = PER
    anywhere = pl.BlockSpec(memory_space=pl.ANY)
    dma = pltpu.SemaphoreType.DMA
    scratch = [
        pltpu.SMEM((2, nbatch), jnp.int32),
        pltpu.SMEM((1, nbatch), jnp.int32),
        pltpu.VMEM(basis.shape, B16),
        pltpu.VMEM(wpot.shape, F32),
        pltpu.VMEM(xc.shape, F32),
        pltpu.VMEM((1, nocc), F32),
        pltpu.VMEM(evirt.shape, F32),
        pltpu.VMEM((rows, nocc), B16),
        pltpu.VMEM((nbatch, points), F32),
        pltpu.VMEM((WIN, WIN), B16),
        pltpu.VMEM((WIN, nocc), B16),
        pltpu.VMEM((nocc, WIN), B16),
        pltpu.VMEM((nbatch // per, TALL, per * points), B16),
        pltpu.VMEM((WIN, WIN), F32),
        pltpu.VMEM((8, SL, 128), HAM_LINK),
        pltpu.VMEM((8, SL // 2, 128), HAM_LINK),
        pltpu.VMEM((8, SL, 128), HAM_LINK),
        pltpu.VMEM((8, SL // 2, 128), HAM_LINK),
        pltpu.VMEM((SL, 128 * nz), B16),
        pltpu.VMEM((nx, nz, 2, BLK, WIN), B16),
        pltpu.VMEM((8, nx * WIN), F32),
        pltpu.VMEM((nocc, 128), F32),
        pltpu.VMEM((nx, 8, 16, 128), VIRT_LINK),
        pltpu.VMEM((nx, ny, 8 // ny, 16, 128), VIRT_LINK),
        pltpu.VMEM((nx, 8, 16, 128), B16),
        pltpu.VMEM((HALVES, nz, SL // HALVES, 128), COEF_LINK),
        pltpu.VMEM((HALVES, nz, SL // HALVES, 128), COEF_LINK),
        pltpu.VMEM((8, HALVES, SL // HALVES, 128), B16),
        pltpu.VMEM((8, HALVES, SL // HALVES // 2, 128), B16),
        pltpu.VMEM((2, HALVES, SL // HALVES // 2, 128), B16),
        pltpu.VMEM((nx, BLK, WIN), B16),
        pltpu.VMEM(virt.shape, B16),
        dma((12,)),
        dma, dma((2,)),
        dma, dma((nz // 2 + 2,)),
        dma((2,)), dma((2, nz // 2 + 2)),
        dma, dma((3,)),
        dma, dma((4,)),
        dma, dma,
        dma((2,)), dma((2,)),
        dma, dma,
        dma, dma((4,)),
        dma, dma((4,)),
        dma, dma((HALVES,)),
        dma((2,)), dma((2,)),
        dma, dma((3,)),
    ]
    coef, potential = pl.pallas_call(
        functools.partial(kernel, topo),
        out_shape=(
            jax.ShapeDtypeStruct((rows, nocc), B16),
            jax.ShapeDtypeStruct((nbatch, points), F32),
        ),
        in_specs=[pl.BlockSpec(memory_space=pltpu.HBM)] * 9,
        out_specs=(anywhere, anywhere),
        scratch_shapes=scratch,
        compiler_params=pltpu.CompilerParams(collective_id=0, has_side_effects=True, vmem_limit_bytes=24 << 20),
        name="dfpt_cycle",
    )(*(
        pltpu.with_memory_space_constraint(array, pltpu.HBM)
        for array in (
            basis, blocks.T, counts.reshape(1, -1), wpot, xc, occ, virt,
            eocc.reshape(1, -1), evirt,
        )
    ))
    return pl.pallas_call(
        hand_out,
        out_shape=(
            jax.ShapeDtypeStruct(coef.shape, coef.dtype),
            jax.ShapeDtypeStruct(potential.shape, potential.dtype),
        ),
        in_specs=[anywhere] * 2,
        out_specs=(anywhere, anywhere),
        scratch_shapes=[dma((2,))],
        compiler_params=pltpu.CompilerParams(vmem_limit_bytes=1 << 20),
        name="hand_out",
    )(coef, potential)


def hand_out(coef, potential, coef_out, potential_out, sems):
    first = pltpu.make_async_copy(coef, coef_out, sems.at[0])
    second = pltpu.make_async_copy(potential, potential_out, sems.at[1])
    first.start()
    second.start()
    first.wait()
    second.wait()


def solution(mesh):
    side = 1
    while 2 * side * side < mesh.shape["grid"]:
        side += 1
    topo = (mesh.shape["tile"], side, side)
    in_specs = (
        P(("grid", "tile"), None, None),
        P(("grid", "tile"), None),
        P(("grid", "tile")),
        P(("grid", "tile"), None),
        P(("grid", "tile"), None),
        P("grid", None),
        P("grid", "tile"),
        P(),
        P("tile"),
    )
    out_specs = (P("grid", None), P(("grid", "tile"), None))
    return jax.shard_map(
        functools.partial(per_device, topo),
        mesh=mesh, in_specs=in_specs, out_specs=out_specs, check_vma=False,
    )
```

```python
import functools

import jax
import jax.numpy as jnp
from jax import lax
from jax.experimental import pallas as pl
from jax.experimental.pallas import tpu as pltpu
from jax.sharding import PartitionSpec as P

MESH = pl.DeviceIdType.MESH
B16 = jnp.bfloat16
F32 = jnp.float32
HAM_LINK = jnp.bfloat16
VIRT_LINK = jnp.bfloat16
COEF_LINK = jnp.bfloat16
NT = (((1,), (1,)), ((), ()))
NN = (((1,), (0,)), ((), ()))
BLK = 64
WIN = 256
SL = 64
PER = 8
HALVES = 1
TALL = 192


def dot(a, b, dims=NN):
    return lax.dot_general(a, b, dims, preferred_element_type=F32)


def split(a):
    high = a.astype(B16)
    return high, (a - high.astype(F32)).astype(B16)


def kernel(
    topo, basis_in, blocks_in, counts_in, wpot_in, xc_in, occ, virt_in, eocc_in, evirt_in,
    coef_out, dens_out,
    blocks, counts, basis, wpot, xc, eocc, evirt, coef, dens, gmat,
    occw, occt, bw, mat, ps, po, rb, ro, hz, v2, evb, eot, ws, wr, rz, cs, cr, cw, cf, cp, staged, virt,
    sl, sa, ra, sv1, rv1, rv2, rvf, sv3, rv3, se, re,
    rbs, rh, rw, rr, rc, rd, ss, rs,
):
    nx, ny, nz = topo
    nq = ny * nz
    g = lax.axis_index("grid")
    t = lax.axis_index("tile")
    c = g % 2
    q = g // 2
    z = q % nz
    y = q // nz
    gother = (g + 2 * nq - 1 + 2 * c) % (2 * nq)
    qup = (q + 1) % nq
    qdown = (q + nq - 1) % nq
    qother = (q + nq - 1 + 2 * c) % nq
    s_me = t * 2 + c
    groups, _, span = bw.shape
    per = span // WIN
    nbatch = groups * per
    third = nbatch // 3

    def local(src, dst, sem):
        copy = pltpu.make_async_copy(src, dst, sem)
        copy.start()
        return copy

    def zring(d):
        zz = (z + d) % nz
        return zz, 2 * (y * nz + zz) + c

    def yring(d):
        yy = (y + d) % ny
        return yy, 2 * (yy * nz + z) + c

    def push(src, dst, send, recv, gg, tt):
        pltpu.make_async_remote_copy(
            src_ref=src, dst_ref=dst, send_sem=send, recv_sem=recv,
            device_id=(gg, tt), device_id_type=MESH,
        ).start()

    def bytes_of(ref, sem):
        pltpu.make_async_copy(ref, ref, sem).wait()

    def vstart(zz):
        return pl.multiple_of(WIN * zz - 128 * (zz // (nz - 1)), 128)

    def outward(n):
        return sorted(range(1, n), key=lambda d: (min(d, n - d), d))

    znear, ynear = outward(nz), outward(ny)
    zfar, yfar = znear[::-1], ynear[::-1]
    xnear = [0] + outward(nx)
    xfar = xnear[::-1]

    bar = pltpu.get_barrier_semaphore()
    own_chip = [(dc, dt) for dc in range(2) for dt in range(nx) if (dc, dt) != (0, 0)]
    for dc, dt in own_chip:
        pl.semaphore_signal(
            bar, inc=1, device_id=(2 * q + (c + dc) % 2, (t + dt) % nx), device_id_type=MESH
        )
    for qq in (qup, qdown):
        for cc in range(2):
            for tt in range(nx):
                pl.semaphore_signal(bar, inc=1, device_id=(2 * qq + cc, tt), device_id_type=MESH)
    for d in range(1, nz):
        pl.semaphore_signal(bar, inc=1, device_id=(zring(d)[1], t), device_id_type=MESH)
    for d in range(1, ny):
        pl.semaphore_signal(bar, inc=1, device_id=(yring(d)[1], t), device_id_type=MESH)

    own_rows = pl.ds(pl.multiple_of(BLK * c, BLK), BLK)
    far_rows = slice(2 * BLK, 3 * BLK)
    load_o = local(occ, occw.at[own_rows], sl.at[5])
    load_u = local(virt_in, virt, sl.at[11])
    loads = [
        local(basis_in.at[pl.ds(third * k, third)], basis.at[pl.ds(third * k, third)], sl.at[k])
        for k in range(3)
    ]
    load_b = local(blocks_in, blocks, sl.at[8])
    load_n = local(counts_in, counts, sl.at[9])
    load_w = local(wpot_in, wpot, sl.at[3])
    load_v = local(virt_in.at[:, pl.ds(vstart(z), WIN)], v2.at[t, z, c], sl.at[4])

    pl.semaphore_wait(bar, len(own_chip) + 4 * nx + nz - 1 + ny - 1)

    sib = 2 * q + 1 - c
    load_o.wait()
    push(occw.at[own_rows], occw.at[far_rows], sa, ra.at[1], gother, t)
    push(occw.at[own_rows], occw.at[own_rows], sa, ra.at[0], sib, t)
    load_u.wait()
    right, left, across = (t + 1) % nx, (t + nx - 1) % nx, (t + 2) % nx
    steps = [[0], [1], [nz - 1]] + [znear[n : n + 2] for n in range(2, nz - 1, 2)]
    group_of = {d: n for n, ds in enumerate(steps) for d in ds}
    before = zring(nz - 1)
    chunk = virt.at[:, pl.ds(vstart(before[0]), WIN)]
    for k, to in enumerate((right, left)):
        push(chunk, staged.at[t], sv3, rv2.at[k, 1], g, to)
    for d in [nz // 2, 1] + znear[2:-1] + [nz - 1]:
        zz, gg = zring(d)
        group = group_of[nz - d]
        push(virt.at[:, pl.ds(vstart(zz), WIN)], v2.at[t, z, c], sv1, rv1.at[group], gg, t)
    load_eo = local(eocc_in, eocc, sl.at[6])
    load_ev = local(evirt_in, evirt, sl.at[7])
    load_x = local(xc_in, xc, sl.at[10])
    mat[...] = jnp.zeros_like(mat)
    occw[3 * BLK : WIN, :] = jnp.zeros((BLK, occw.shape[1]), B16)

    row = lax.broadcasted_iota(jnp.int32, (TALL, 128), 0)
    col = lax.broadcasted_iota(jnp.int32, (TALL, 128), 1)
    lane = lax.broadcasted_iota(jnp.int32, (1, WIN), 1)
    load_w.wait()
    load_b.wait()
    load_n.wait()

    def integrate(n, carry):
        wides, scaled = [], []
        for j in range(per):
            b = per * n + j
            first = (BLK * (blocks[0, b] + c + 2)) % (3 * BLK)
            second = (BLK * (blocks[1, b] + c + 2)) % (3 * BLK)
            target = jnp.where(col < BLK, col + first, col - BLK + second)
            pick = jnp.where(row == target, 1.0, 0.0).astype(B16)
            spread = dot(pick, basis[b], NT)
            wide = spread.astype(B16)
            bw[n, :, WIN * j : WIN * j + WIN] = wide
            weight = jnp.where(lane < counts[0, b], wpot[pl.ds(b, 1), :], 0.0)
            wides.append(wide)
            scaled.append((spread * weight).astype(B16))
        mat[0:TALL, 0:TALL] += dot(jnp.concatenate(scaled, axis=1), jnp.concatenate(wides, axis=1), NT)
        return carry

    for k in range(3):
        loads[k].wait()
        lax.fori_loop(groups * k // 3, groups * (k + 1) // 3, integrate, 0)
        if k == 0:
            load_v.wait()
            for n, to in enumerate((right, left)):
                push(v2.at[t, z, c], v2.at[t, z, c], sv3, rv2.at[n, 0], g, to)

    bytes_of(occw.at[pl.ds(pl.multiple_of(BLK * (1 - c), BLK), BLK)], ra.at[0])
    bytes_of(occw.at[far_rows], ra.at[1])
    occt[...] = jnp.transpose(occw[...].astype(F32)).astype(B16)
    high, low = split(mat[...])
    part = dot(occt[...], high) + dot(occt[...], low)
    half_lane = lax.broadcasted_iota(jnp.int32, (SL // 2, 128), 1) < BLK
    for s in range(2 * nx):
        rows = part[SL * s : SL * s + SL]
        ps[s] = rows[:, 0:128].astype(HAM_LINK)
        top, bottom = rows[0 : SL // 2, 128:256], rows[SL // 2 : SL, 128:256]
        po[s] = jnp.where(half_lane, top, pltpu.roll(bottom, BLK, 1)).astype(HAM_LINK)


    def along_x(n):
        ds = steps[n]
        bytes_of(v2.at[t, 0 : len(ds), c], rv1.at[n])
        for d in ds:
            mine = v2.at[t, (z + d) % nz, c]
            push(mine, mine, sv3, rv2.at[0, n], g, right)
            push(mine, mine, sv3, rv2.at[1, n], g, left)

    slot = 4 * c + t
    rb[slot] = ps[s_me]

    def give_ham():
        for dt in xfar:
            tt = (t + dt) % nx
            for cc in range(2):
                push(po.at[tt * 2 + cc], ro.at[slot], sa, rbs.at[1], 2 * qother + cc, tt)
            for dc in range(2):
                if dc or dt:
                    cc = (c + dc) % 2
                    push(ps.at[tt * 2 + cc], rb.at[slot], sv1, rbs.at[0], 2 * q + cc, tt)

    give_ham()
    for k, (frm, to) in enumerate(((left, right), (right, left))):
        bytes_of(staged.at[0], rv2.at[k, 1])
        if k == 1:
            push(staged.at[frm], staged.at[frm], sv3, rvf.at[0], g, to)
        push(staged.at[frm], v2.at[frm, z, c], ss, rs.at[k], before[1], t)
    for n in range(2, len(steps)):
        along_x(n)
    bytes_of(staged.at[0], rvf.at[0])
    push(staged.at[across], v2.at[across, z, c], ss, rs.at[2], before[1], t)
    load_eo.wait()
    load_x.wait()
    load_ev.wait()
    eot[...] = jnp.transpose(jnp.broadcast_to(eocc[...], (128, eocc.shape[1])))
    evb[:, pl.ds(pl.multiple_of(WIN * t, WIN), WIN)] = jnp.broadcast_to(
        evirt[pl.ds(vstart(z), WIN)].reshape(1, WIN), (8, WIN)
    )
    mine_e = evb.at[:, pl.ds(pl.multiple_of(WIN * t, WIN), WIN)]
    for d in range(1, nx):
        push(mine_e, mine_e, se, re, g, (t + d) % nx)

    bytes_of(rb.at[0:7], rbs.at[0])
    bytes_of(ro, rbs.at[1])
    ham = rb[0].astype(F32)
    for k in range(1, 8):
        ham = ham + rb[k].astype(F32)
    above = ro[0].astype(F32)
    below = ro[4].astype(F32)
    for k in range(1, 4):
        above = above + ro[k].astype(F32)
        below = below + ro[4 + k].astype(F32)
    halo = jnp.concatenate([
        jnp.where(half_lane, below, pltpu.roll(above, BLK, 1)),
        jnp.where(half_lane, pltpu.roll(below, BLK, 1), above),
    ], axis=0)
    ham = ham + halo
    zcols = lambda zz: pl.ds(pl.multiple_of(128 * zz, 128), 128)
    hz[:, zcols(z)] = ham.astype(B16)
    for d in zfar:
        push(hz.at[:, zcols(z)], hz.at[:, zcols(z)], sv1, rh, zring(d)[1], t)
    bytes_of(v2.at[t, 0, c], rv1.at[1])
    push(v2.at[t, :, c], v2.at[t, :, c], sv3, rv3.at[0], sib, t)

    def to_sibling(tt, n, ds):
        for d in ds:
            block = v2.at[tt, (z + d) % nz, c]
            push(block, block, sv3, rv3.at[n], sib, t)

    rightward = (0, nz - 2)
    for n, ds in enumerate(steps):
        if n == 1:
            continue
        for k, (frm, to) in enumerate(((left, right), (right, left))):
            bytes_of(v2.at[frm, 0 : len(ds), c], rv2.at[k, n])
            for d in ds:
                if (d in rightward) == (k == 0):
                    theirs = v2.at[frm, (z + d) % nz, c]
                    push(theirs, theirs, sv3, rvf.at[2 if n == len(steps) - 1 else 1], g, to)
            to_sibling(frm, 1 + k, ds)
    for k, frm in enumerate((left, right)):
        bytes_of(v2.at[frm, 0, c], rs.at[k])
        to_sibling(frm, 1 + k, [1])
    bytes_of(hz.at[:, 0 : 128 * (nz - 1)], rh)

    share = 8 // ny

    def virtual(tt, n):
        bytes_of(v2.at[tt, :, 1 - c], rv3.at[n])
        part = dot(hz[...], v2[tt].reshape(nz * 128, WIN))
        for k in range(8):
            i, a = 16 * (k // 2), 128 * (k % 2)
            ws[n, k] = part[i : i + 16, a : a + 128].astype(VIRT_LINK)
        wr[n, y] = ws[n, pl.ds(y * share, share)]
        for d in yfar:
            yy, gg = yring(d)
            push(ws.at[n, pl.ds(yy * share, share)], wr.at[n, y], sv1, rw.at[n], gg, t)

    def rotate(tt, n):
        bytes_of(wr.at[n, 0 : ny - 1], rw.at[n])
        for h in range(share):
            k = y * share + h
            total = wr[n, 0, h].astype(F32)
            for yy in range(1, ny):
                total = total + wr[n, yy, h].astype(F32)
            i = pl.multiple_of(SL * s_me + 16 * (k // 2), 16)
            a = pl.multiple_of(WIN * tt + 128 * (k % 2), 128)
            gap = eot[pl.ds(i, 16), 0:1] - evb[0:1, pl.ds(a, 128)]
            repeat = lax.broadcasted_iota(jnp.int32, (16, 128), 1) * 0 + k % 2 < z // (nz - 1)
            rz[n, k] = jnp.where(repeat, 0.0, total / gap).astype(B16)
        mine = rz.at[n, pl.ds(y * share, share)]
        for d in yfar:
            push(mine, mine, sv1, rr.at[n], yring(d)[1], t)

    def respond_to(tt, n):
        bytes_of(rz.at[n, 0 : (ny - 1) * share], rr.at[n])
        turn = jnp.concatenate([
            jnp.concatenate([rz[n, k], rz[n, k + 1]], axis=1) for k in range(0, 8, 2)
        ], axis=0)
        return dot(turn, v2[tt].reshape(nz * 128, WIN), NT)

    virtual(t, 0)
    last = steps[-1]
    bytes_of(v2.at[across, 0, c], rs.at[2])
    bytes_of(v2.at[across, 0 : nz - 1 - len(last), c], rvf.at[1])
    to_sibling(across, 3, [d for d in range(nz) if d not in last])
    virtual(left, 1)
    bytes_of(v2.at[across, 0 : len(last), c], rvf.at[2])
    to_sibling(across, 3, last)
    virtual(right, 2)
    virtual(across, 3)
    bytes_of(evb.at[:, 0 : WIN * (nx - 1)], re)
    tiles = (t, left, right, across)
    for n in range(nx - 1):
        rotate(tiles[n], n)
    rotate(tiles[nx - 1], nx - 1)
    part = respond_to(tiles[0], 0)
    for n in range(1, nx - 1):
        part += respond_to(tiles[n], n)
    part += respond_to(tiles[nx - 1], nx - 1)
    rise = SL // HALVES
    for h in range(HALVES):
        for k in range(nz):
            cs[h, k] = part[rise * h : rise * (h + 1), 128 * k : 128 * k + 128].astype(COEF_LINK)
    for h in range(HALVES):
        for d in zfar:
            zz, gg = zring(d)
            push(cs.at[h, zz], cr.at[h, z], sv1, rc.at[h], gg, t)
    quarter_lane = lax.broadcasted_iota(jnp.int32, (rise // 2, 128), 1) < BLK
    for h in range(HALVES):
        cr[h, z] = cs[h, z]
        bytes_of(cr.at[h, 0 : nz - 1], rc.at[h])
        done = cr[h, 0].astype(F32)
        for k in range(1, nz):
            done = done + cr[h, k].astype(F32)
        cw[s_me, h] = done.astype(B16)
        top, bottom = done[0 : rise // 2], done[rise // 2 : rise]
        cp[0, h] = jnp.where(quarter_lane, pltpu.roll(top, BLK, 1), bottom).astype(B16)
        cp[1, h] = jnp.where(quarter_lane, top, pltpu.roll(bottom, BLK, 1)).astype(B16)
        for dt in xfar:
            tt = (t + dt) % nx
            push(cp.at[0, h], cf.at[s_me, h], sa, rd.at[1], 2 * qup, tt)
            push(cp.at[1, h], cf.at[s_me, h], sa, rd.at[1], 2 * qdown + 1, tt)
            for dc in range(2):
                if dc or dt:
                    mine = cw.at[s_me, h]
                    push(mine, mine, sv1, rd.at[0], 2 * q + (c + dc) % 2, tt)
    bytes_of(cw.at[0:7], rd.at[0])
    near = cw[...].reshape(8 * SL, 128)
    krow = lax.broadcasted_iota(jnp.int32, (BLK, 128), 0)
    kcol = lax.broadcasted_iota(jnp.int32, (BLK, 128), 1)
    pick = jnp.where(kcol == krow + BLK * c, 1.0, 0.0).astype(B16)
    coef[...] = dot(pick, near, NT).astype(B16)
    give_c = local(coef, coef_out, sl.at[0])
    gmat[:, 0:128] = dot(occw[...], near).astype(B16)
    bytes_of(cf, rd.at[1])
    pieces = []
    for k in range(8):
        for h in range(HALVES):
            packed = cf[k, h]
            pieces += [packed, pltpu.roll(packed.astype(F32), BLK, 1).astype(B16)]
    far = jnp.concatenate(pieces, axis=0)
    gmat[:, 128:256] = dot(occw[...], far).astype(B16)

    def respond(n, carry):
        wide = bw[n]
        resp = dot(gmat[0:TALL, 0:TALL], wide)
        total = jnp.sum(resp * wide.astype(F32), axis=0, keepdims=True)
        for j in range(per):
            b = per * n + j
            value = xc[pl.ds(b, 1), :] * (4.0 * total[:, WIN * j : WIN * j + WIN])
            dens[pl.ds(b, 1), :] = jnp.where(lane < counts[0, b], value, 0.0)
        return carry

    lax.fori_loop(0, groups, respond, 0)
    give_d = local(dens, dens_out, sl.at[1])
    bytes_of(v2.at[0, :, 0], sa)
    bytes_of(v2.at[:, 0 : nz - 1, 0], sv1)
    bytes_of(v2.at[:, 0 : nz - 1], sv3)
    bytes_of(v2.at[0:3, 0, 0], ss)
    bytes_of(evb.at[:, 0 : WIN * (nx - 1)], se)
    give_c.wait()
    give_d.wait()


def per_device(topo, basis, blocks, counts, wpot, xc, occ, virt, eocc, evirt):
    nx, ny, nz = topo
    nbatch, points, columns = basis.shape
    rows, nocc = occ.shape
    per = PER
    anywhere = pl.BlockSpec(memory_space=pl.ANY)
    dma = pltpu.SemaphoreType.DMA
    scratch = [
        pltpu.SMEM((2, nbatch), jnp.int32),
        pltpu.SMEM((1, nbatch), jnp.int32),
        pltpu.VMEM(basis.shape, B16),
        pltpu.VMEM(wpot.shape, F32),
        pltpu.VMEM(xc.shape, F32),
        pltpu.VMEM((1, nocc), F32),
        pltpu.VMEM(evirt.shape, F32),
        pltpu.VMEM((rows, nocc), B16),
        pltpu.VMEM((nbatch, points), F32),
        pltpu.VMEM((WIN, WIN), B16),
        pltpu.VMEM((WIN, nocc), B16),
        pltpu.VMEM((nocc, WIN), B16),
        pltpu.VMEM((nbatch // per, TALL, per * points), B16),
        pltpu.VMEM((WIN, WIN), F32),
        pltpu.VMEM((8, SL, 128), HAM_LINK),
        pltpu.VMEM((8, SL // 2, 128), HAM_LINK),
        pltpu.VMEM((8, SL, 128), HAM_LINK),
        pltpu.VMEM((8, SL // 2, 128), HAM_LINK),
        pltpu.VMEM((SL, 128 * nz), B16),
        pltpu.VMEM((nx, nz, 2, BLK, WIN), B16),
        pltpu.VMEM((8, nx * WIN), F32),
        pltpu.VMEM((nocc, 128), F32),
        pltpu.VMEM((nx, 8, 16, 128), VIRT_LINK),
        pltpu.VMEM((nx, ny, 8 // ny, 16, 128), VIRT_LINK),
        pltpu.VMEM((nx, 8, 16, 128), B16),
        pltpu.VMEM((HALVES, nz, SL // HALVES, 128), COEF_LINK),
        pltpu.VMEM((HALVES, nz, SL // HALVES, 128), COEF_LINK),
        pltpu.VMEM((8, HALVES, SL // HALVES, 128), B16),
        pltpu.VMEM((8, HALVES, SL // HALVES // 2, 128), B16),
        pltpu.VMEM((2, HALVES, SL // HALVES // 2, 128), B16),
        pltpu.VMEM((nx, BLK, WIN), B16),
        pltpu.VMEM(virt.shape, B16),
        dma((12,)),
        dma, dma((2,)),
        dma, dma((nz // 2 + 2,)),
        dma((2, nz // 2 + 2)), dma((3,)),
        dma, dma((4,)),
        dma, dma,
        dma((2,)), dma, dma((4,)), dma((4,)), dma((HALVES,)), dma((2,)),
        dma, dma((3,)),
    ]
    coef, potential = pl.pallas_call(
        functools.partial(kernel, topo),
        out_shape=(
            jax.ShapeDtypeStruct((rows, nocc), B16),
            jax.ShapeDtypeStruct((nbatch, points), F32),
        ),
        in_specs=[pl.BlockSpec(memory_space=pltpu.HBM)] * 9,
        out_specs=(anywhere, anywhere),
        scratch_shapes=scratch,
        compiler_params=pltpu.CompilerParams(collective_id=0, has_side_effects=True, vmem_limit_bytes=24 << 20),
        name="dfpt_cycle",
    )(*(
        pltpu.with_memory_space_constraint(array, pltpu.HBM)
        for array in (
            basis, blocks.T, counts.reshape(1, -1), wpot, xc, occ, virt,
            eocc.reshape(1, -1), evirt,
        )
    ))
    return pl.pallas_call(
        hand_out,
        out_shape=(
            jax.ShapeDtypeStruct(coef.shape, coef.dtype),
            jax.ShapeDtypeStruct(potential.shape, potential.dtype),
        ),
        in_specs=[anywhere] * 2,
        out_specs=(anywhere, anywhere),
        scratch_shapes=[dma((2,))],
        compiler_params=pltpu.CompilerParams(vmem_limit_bytes=1 << 20),
        name="hand_out",
    )(coef, potential)


def hand_out(coef, potential, coef_out, potential_out, sems):
    first = pltpu.make_async_copy(coef, coef_out, sems.at[0])
    second = pltpu.make_async_copy(potential, potential_out, sems.at[1])
    first.start()
    second.start()
    first.wait()
    second.wait()


def solution(mesh):
    side = 1
    while 2 * side * side < mesh.shape["grid"]:
        side += 1
    topo = (mesh.shape["tile"], side, side)
    in_specs = (
        P(("grid", "tile"), None, None),
        P(("grid", "tile"), None),
        P(("grid", "tile")),
        P(("grid", "tile"), None),
        P(("grid", "tile"), None),
        P("grid", None),
        P("grid", "tile"),
        P(),
        P("tile"),
    )
    out_specs = (P("grid", None), P(("grid", "tile"), None))
    return jax.shard_map(
        functools.partial(per_device, topo),
        mesh=mesh, in_specs=in_specs, out_specs=out_specs, check_vma=False,
    )
```
